128 devices in a mesh: leaf: 32 (over z, y, core), rows: 4 (over x).
Axes of the slice: x: 4, y: 4, z: 4, core: 2. Of those that a mesh axis runs over, the one named last changes fastest.
Arguments:
- child_update: float32 [32, 512, 512], P('leaf', 'rows'), as said below
- block_maps: int32 [3, 32, 4], replicated, may hold values from 0 to 11, as said below
- sep_share: float32 [32, 3, 1024, 1024], P('leaf', None, 'rows'), as said below
- coupling_share: float32 [32, 3, 512, 1024], P('leaf', None, 'rows')
Outputs:
- diag_factor: float32 [32, 3, 1024, 1024], P('leaf', None, 'rows')
- below_factor: float32 [32, 3, 512, 1024], P('leaf', None, 'rows')
- top_update: float32 [32, 512, 512], P('leaf', 'rows')
The draws below stay inside these ranges and needn't reach their ends.
Inputs may be any that keep to these rules, and one draw needn't show every extreme that they name: Each row block_maps[k, c] names 4 different front blocks; at every level k, the rows 2g and 2g+1 together name every block from 8 on. At level k only the rows c < 32 / 2^k are used. `child_update`: Symmetric. `sep_share`: symmetric in its last two dimensions.
All inputs are finite; a program needn't handle non-finite values.
Results may differ from the reference program's by a relative error of at most 0.00012.
Values sent between devices are 32-bit elements; how exact they have to be, the bound alone decides.
No kernel may reach another device: no remote copies, remote signals or barrier semaphores. Data moves between devices by JAX's collectives and lax.ppermute only.
A program may use at most 192 MiB of HBM per device.

```python
import math
import jax
import jax.numpy as jnp
from jax import lax

BLK = 128
SEP = 1024
UPD = 512
LEVELS = 3
LEAVES = 32
FRONT = 1536


def symmetric_noise(noise_key, shape, spread):
    values = jax.random.normal(noise_key, shape, jnp.float32) * spread
    return (values + jnp.swapaxes(values, -1, -2)) * 0.5


def share_scale():
    return 2.0 ** (-(jnp.arange(LEVELS, dtype=jnp.float32) + 1.0))


def grid_operator(key, lead, order, kappa_low, kappa_high):
    noise_key, right_key, down_key, kappa_key = jax.random.split(key, 4)
    width = BLK // 4
    low_log = math.log(0.5)
    high_log = math.log(2.0)
    shape = lead + (order,)
    position = jnp.arange(order, dtype=jnp.int32)
    has_right = ((position + 1) % width != 0) & (position + 1 < order)
    has_down = position + width < order
    c_right = jnp.exp(jax.random.uniform(right_key, shape, jnp.float32, low_log, high_log)) * has_right.astype(jnp.float32)
    c_down = jnp.exp(jax.random.uniform(down_key, shape, jnp.float32, low_log, high_log)) * has_down.astype(jnp.float32)
    from_left = jnp.concatenate([jnp.zeros(lead + (1,), jnp.float32), c_right[..., :-1]], axis=-1)
    from_above = jnp.concatenate([jnp.zeros(lead + (width,), jnp.float32), c_down[..., :-width]], axis=-1)
    degree = c_right + c_down + from_left + from_above
    kappa = jax.random.uniform(kappa_key, shape, jnp.float32, kappa_low, kappa_high)
    row_pos = position[:, None]
    col_pos = position[None, :]
    stencil = jnp.where(col_pos == row_pos + 1, c_right[..., :, None], 0.0) + jnp.where(row_pos == col_pos + 1, c_right[..., None, :], 0.0) + jnp.where(col_pos == row_pos + width, c_down[..., :, None], 0.0) + jnp.where(row_pos == col_pos + width, c_down[..., None, :], 0.0)
    noise = symmetric_noise(noise_key, shape + (order,), 0.14142136 / math.sqrt(order))
    diagonal = jnp.where(row_pos == col_pos, (degree + kappa + 0.3)[..., :, None], 0.0)
    return noise - stencil + diagonal


def draw_child_update(key, part):
    return grid_operator(key, (LEAVES,), UPD, 3.5, 5.0)


def draw_sep_share(key, part):
    operator = grid_operator(key, (LEAVES, LEVELS), SEP, 0.1, 0.6)
    return operator * share_scale()[None, :, None, None]


def draw_coupling_share(key, part):
    scale = share_scale()[None, :, None, None] * (0.7778175 / math.sqrt(SEP))
    values = jax.random.normal(key, (LEAVES, LEVELS, UPD, SEP), jnp.float32)
    return values * scale


def draw_block_maps(key, part):
    blocks_front = (SEP + UPD) // BLK
    blocks_child = UPD // BLK
    first_update = SEP // BLK
    pair_keys = jax.random.split(key, LEVELS * (LEAVES // 2))

    def pair_maps(pair_key):
        left_key, right_key = jax.random.split(pair_key)
        positions = jnp.arange(blocks_front, dtype=jnp.int32)
        left_map = jax.random.permutation(left_key, blocks_front)[:blocks_child].astype(jnp.int32)
        covered = jnp.sum((left_map[:, None] == positions[None, :]).astype(jnp.int32), axis=0)
        needed = ((positions >= first_update) & (covered == 0)).astype(jnp.int32)
        score = jax.random.permutation(right_key, blocks_front).astype(jnp.int32) + blocks_front * needed
        right_map = jnp.argsort(-score, stable=True)[:blocks_child].astype(jnp.int32)
        return jnp.stack([left_map, right_map])
    maps_all = jax.vmap(pair_maps)(pair_keys)
    return maps_all.reshape(LEVELS, LEAVES, blocks_child)


def setup_inputs(seed: int = 0) -> dict:
    arg_keys = jax.random.split(jax.random.key(seed), 5)
    return {
        "child_update": draw_child_update(jax.random.fold_in(arg_keys[4], 71), 0),
        "block_maps": draw_block_maps(jax.random.fold_in(arg_keys[4], 71), 0),
        "sep_share": draw_sep_share(jax.random.fold_in(arg_keys[4], 71), 0),
        "coupling_share": draw_coupling_share(jax.random.fold_in(arg_keys[4], 71), 0),
    }


highest = lax.Precision.HIGHEST

def block_cholesky(matrix):
    order = matrix.shape[-1]
    if order <= 512:
        return jnp.linalg.cholesky(matrix, symmetrize_input=False)
    half = order // 2
    top_factor = block_cholesky(matrix[..., :half, :half])
    lower_panel = lax.linalg.triangular_solve(top_factor, matrix[..., half:, :half], left_side=False, lower=True, transpose_a=True)
    remainder = matrix[..., half:, half:] - jnp.einsum('...ik,...jk->...ij', lower_panel, lower_panel, precision=highest)
    bottom_factor = block_cholesky(remainder)
    upper_zero = jnp.zeros(matrix.shape[:-2] + (half, order - half), jnp.float32)
    top_rows = jnp.concatenate([top_factor, upper_zero], axis=-1)
    bottom_rows = jnp.concatenate([lower_panel, bottom_factor], axis=-1)
    return jnp.concatenate([top_rows, bottom_rows], axis=-2)

def sym_cholesky(matrix):
    return block_cholesky((matrix + jnp.swapaxes(matrix, -1, -2)) * 0.5)

def assemble(children, level_maps):
    group_count = children.shape[0]
    blocks_child = UPD // BLK
    blocks_front = FRONT // BLK
    selector = (level_maps[:, :, None, :] == jnp.arange(blocks_front, dtype=jnp.int32)[:, None]).astype(jnp.float32)
    tiles = children.reshape(group_count, 2, blocks_child, BLK, blocks_child, BLK)
    placed = jnp.einsum('gcpm,gcmanb->gcpanb', selector, tiles, precision=highest)
    assembled = jnp.einsum('gcqn,gcpanb->gpaqb', selector, placed, precision=highest)
    return assembled.reshape(group_count, FRONT, FRONT)

def reference(child_update, block_maps, sep_share, coupling_share):
    updates = child_update
    diag_parts = []
    below_parts = []
    for level_index in range(LEVELS):
        size_group = 2 ** (level_index + 1)
        groups = LEAVES // size_group
        sep_orig = jnp.sum(sep_share[:, level_index].reshape(groups, size_group, SEP, SEP), axis=1)
        cpl_orig = jnp.sum(coupling_share[:, level_index].reshape(groups, size_group, UPD, SEP), axis=1)
        level_maps = block_maps[level_index, :2 * groups].reshape(groups, 2, UPD // BLK)
        front_whole = assemble(updates.reshape(groups, 2, UPD, UPD), level_maps)
        front_pivot = front_whole[:, :SEP, :SEP] + sep_orig
        front_below = front_whole[:, SEP:, :SEP] + cpl_orig
        front_trail = front_whole[:, SEP:, SEP:]
        pivot_factor = sym_cholesky(front_pivot)
        below_rows = lax.linalg.triangular_solve(pivot_factor, front_below, left_side=False, lower=True, transpose_a=True)
        updates = front_trail - jnp.einsum('gik,gjk->gij', below_rows, below_rows, precision=highest)
        diag_parts.append(jnp.repeat(pivot_factor, size_group, axis=0))
        below_parts.append(jnp.repeat(below_rows, size_group, axis=0))
    top_update = jnp.repeat(updates, 2 ** LEVELS, axis=0)
    return (jnp.stack(diag_parts, axis=1), jnp.stack(below_parts, axis=1), top_update)
```

```python
import jax
import jax.numpy as jnp
from jax import lax
from jax.experimental import pallas as pl
from jax.experimental.pallas import tpu as pltpu
from jax.sharding import PartitionSpec as P

BLK = 128
SEP = 1024
UPD = 512
FRONT = SEP + UPD
LEVELS = 3
NSEP = SEP // BLK
NUPD = UPD // BLK
f32 = jnp.float32
bf16 = jnp.bfloat16


def lane_b(x, c):
    return jnp.broadcast_to(x[:, c : c + 1], x.shape)


def sub_b(x, i):
    return jnp.broadcast_to(x[i : i + 1, :], x.shape)


def block_inverse(rows_a):
    groups = BLK // 8
    row = lax.broadcasted_iota(jnp.int32, (8, BLK), 0)
    col = lax.broadcasted_iota(jnp.int32, (8, BLK), 1)
    A = list(rows_a)
    V = [jnp.where(col == row + 8 * g, 1.0, 0.0).astype(f32) for g in range(groups)]
    out = []
    for b in range(groups):
        c0 = 8 * b
        cols = [lane_b(A[b], c0 + j) for j in range(8)]
        d = [[sub_b(cols[j], i) if i >= j else None for j in range(8)] for i in range(8)]
        xs = [sub_b(A[b], i) for i in range(8)]
        ys = [sub_b(V[b], i) for i in range(8)]
        rs = []
        for k in range(8):
            r = lax.rsqrt(d[k][k])
            rs.append(r)
            for i in range(k + 1, 8):
                d[i][k] = d[i][k] * r
            for j in range(k + 1, 8):
                for i in range(j, 8):
                    d[i][j] = d[i][j] - d[i][k] * d[j][k]
            xs[k] = xs[k] * r
            ys[k] = ys[k] * r
            for i in range(k + 1, 8):
                xs[i] = xs[i] - d[i][k] * xs[k]
                ys[i] = ys[i] - d[i][k] * ys[k]
        for g in range(b + 1, groups):
            cg = [lane_b(A[g], c0 + j) for j in range(8)]
            for k in range(8):
                cg[k] = cg[k] * rs[k]
                for i in range(k + 1, 8):
                    cg[i] = cg[i] - d[i][k] * cg[k]
            for k in range(8):
                A[g] = A[g] - cg[k] * xs[k]
                V[g] = V[g] - cg[k] * ys[k]
        y = ys[0]
        for k in range(1, 8):
            y = jnp.where(row == k, ys[k], y)
        out.append(y)
    return out


def split(x):
    hi = x.astype(bf16)
    return hi, (x - hi.astype(f32)).astype(bf16)


def nt(a, b):
    return lax.dot_general(a, b, (((1,), (1,)), ((), ())), preferred_element_type=f32)


def nt3(a_hi, a_lo, b_hi, b_lo):
    return nt(a_hi, b_hi) + (nt(a_hi, b_lo) + nt(a_lo, b_hi))


def blk(i):
    if isinstance(i, int):
        return pl.ds(i * BLK, BLK)
    return pl.ds(pl.multiple_of(i * BLK, BLK), BLK)


def front_body(level, refs):
    if level == 0:
        ids, sep_in, cpl_in, u_in = refs[:4]
        refs = refs[4:]
    else:
        ids, sep_in, cpl_in, own_in, near_in, far_in = refs[:6]
        refs = refs[6:]
    l_out, r_out, u_out, F, C, Ub, Lh, Ll, Lf, T, D, E, Wh, Wl, sem = refs
    rid = ids[8]
    half = ids[9]
    leaves = 2 << level
    sep_piece = 256 // leaves
    cpl_piece = 128 // leaves
    copies = []
    for leaf in range(leaves):
        slot = 0
        for bit in range(level + 1):
            slot += (leaf >> bit & 1) * (leaves >> bit + 1)
        for r in range(4):
            copies.append((sep_in.at[leaf, r], F.at[pl.ds(r * 256 + slot * sep_piece, sep_piece), :]))
            copies.append((cpl_in.at[leaf, r], F.at[pl.ds(SEP + r * BLK + slot * cpl_piece, cpl_piece), :]))
    if level == 0:
        copies.append((u_in, Ub))
    else:
        copies.append((own_in, Ub.at[0]))
        copies.append((near_in, Ub.at[1, pl.ds(pl.multiple_of(half * 256, 256), 256), :]))
        copies.append((far_in, Ub.at[1, pl.ds(pl.multiple_of((1 - half) * 256, 256), 256), :]))
    copies = [pltpu.make_async_copy(s, t, sem.at[n]) for n, (s, t) in enumerate(copies)]
    for c in copies:
        c.start()
    C[...] = jnp.zeros_like(C)
    Lh[...] = jnp.zeros_like(Lh)
    Ll[...] = jnp.zeros_like(Ll)
    for c in copies:
        c.wait()

    def add_block(t, c):
        child = t // 16
        i = t // 4 % 4
        j = t % 4
        mi = ids[4 * child + i]
        mj = ids[4 * child + j]
        part = Ub[child, blk(i), blk(j)]

        @pl.when(mj < NSEP)
        def _():
            F[blk(mi), blk(mj)] += part

        @pl.when((mj >= NSEP) & (mi >= NSEP))
        def _():
            C[blk(jnp.maximum(mi - NSEP, 0)), blk(jnp.maximum(mj - NSEP, 0))] += part

        return c

    lax.fori_loop(0, 32, add_block, 0)
    D[...] = F[:BLK, :BLK]

    def panel(k, lo):
        th, tl = split(T[lo:, :])
        v = nt3(th, tl, Wh[...], Wl[...])
        Lf[lo:, blk(k)] = v
        h, l = split(v)
        Lh[lo:, blk(k)] = h
        Ll[lo:, blk(k)] = l

    def step(k, lo, depth):
        if depth == 0:
            n = 1
            T[...] = F[:, :BLK]
            E[...] = F[blk(1), blk(1)]
        else:
            n = jnp.minimum(k + 1, NSEP - 1)
            panel(k - 1, lo)
            T[lo:, :] = F[lo:, blk(k)] - nt3(
                Lh[lo:, :depth], Ll[lo:, :depth], Lh[blk(k), :depth], Ll[blk(k), :depth]
            )
            nh = Lh[blk(n), :depth]
            nl = Ll[blk(n), :depth]
            E[...] = F[blk(n), blk(n)] - nt3(nh, nl, nh, nl)
        W = jnp.concatenate(block_inverse([D[8 * g : 8 * g + 8, :] for g in range(BLK // 8)]), axis=0)
        wh, wl = split(W)
        Wh[...] = wh
        Wl[...] = wl
        th, tl = split(T[blk(n), :])
        h, l = split(nt3(th, tl, wh, wl))
        D[...] = E[...] - nt3(h, l, h, l)

    step(0, 0, 0)
    lax.fori_loop(1, 4, lambda k, c: (step(k, 0, 512), c)[1], 0)
    lax.fori_loop(4, 8, lambda k, c: (step(k, 384, 1024), c)[1], 0)
    panel(7, 896)
    rh = Lh[SEP:, :]
    rl = Ll[SEP:, :]
    if level == LEVELS - 1:
        mine = pl.ds(pl.multiple_of(rid * BLK, BLK), BLK)
        mine_l = pl.ds(pl.multiple_of(SEP + rid * BLK, BLK), BLK)
        u_out[...] = C[mine, :] - nt3(Lh[mine_l, :], Ll[mine_l, :], rh, rl)
    else:
        u_out[...] = C[...] - nt3(rh, rl, rh, rl)
    rows = pl.ds(pl.multiple_of(rid * 256, 256), 256)
    ri = lax.broadcasted_iota(jnp.int32, (256, SEP), 0) + rid * 256
    ci = lax.broadcasted_iota(jnp.int32, (256, SEP), 1)
    l_out[...] = jnp.where(ri >= ci, Lf[rows, :], 0.0)
    r_out[...] = Lf[pl.ds(pl.multiple_of(SEP + rid * BLK, BLK), BLK), :]


def front(level, ids, sep_in, cpl_in, *updates):
    smem = pl.BlockSpec(memory_space=pltpu.SMEM)
    vmem = pl.BlockSpec(memory_space=pltpu.VMEM)
    hbm = pl.BlockSpec(memory_space=pl.ANY)
    last = level == LEVELS - 1
    copies = 2 * 4 * (2 << level) + 3
    return pl.pallas_call(
        lambda *refs: front_body(level, refs),
        in_specs=[smem] + [hbm] * (2 + len(updates)),
        out_specs=[vmem] * 3,
        out_shape=[
            jax.ShapeDtypeStruct((256, SEP), f32),
            jax.ShapeDtypeStruct((BLK, SEP), f32),
            jax.ShapeDtypeStruct((BLK if last else UPD, UPD), f32),
        ],
        scratch_shapes=[
            pltpu.VMEM((FRONT, SEP), f32),
            pltpu.VMEM((UPD, UPD), f32),
            pltpu.VMEM((2, UPD, UPD), f32),
            pltpu.VMEM((FRONT, SEP), bf16),
            pltpu.VMEM((FRONT, SEP), bf16),
            pltpu.VMEM((FRONT, SEP), f32),
            pltpu.VMEM((FRONT, BLK), f32),
            pltpu.VMEM((BLK, BLK), f32),
            pltpu.VMEM((BLK, BLK), f32),
            pltpu.VMEM((BLK, BLK), bf16),
            pltpu.VMEM((BLK, BLK), bf16),
            pltpu.SemaphoreType.DMA((copies,)),
        ],
        compiler_params=pltpu.CompilerParams(vmem_limit_bytes=48 << 20),
        cost_estimate=pl.CostEstimate(flops=20_000_000_000, transcendentals=0, bytes_accessed=20_000_000),
        name=f"front{level}",
    )(ids, sep_in, cpl_in, *updates)


def swap(x, stride):
    return lax.ppermute(x, "leaf", [(i, i ^ 1 << stride) for i in range(lax.axis_size("leaf"))])


def gather_group(x, level):
    leaves = 2 << level
    groups = [
        [(g * leaves + l) * 4 + r for l in range(leaves) for r in range(4)]
        for g in range(lax.axis_size("leaf") // leaves)
    ]
    return lax.all_gather(x, ("leaf", "rows"), axis_index_groups=groups, axis=0, tiled=False)


def scatter_sum(x, stride, bit):
    half = x.shape[0] // 2
    halves = x.reshape(2, half, x.shape[1])
    keep = lax.dynamic_index_in_dim(halves, bit, 0, keepdims=False)
    give = lax.dynamic_index_in_dim(halves, 1 - bit, 0, keepdims=False)
    return keep + swap(give, stride)


def on_device(child_update, block_maps, sep_share, coupling_share):
    leaf = lax.axis_index("leaf")
    rid = lax.axis_index("rows")
    bits = [leaf >> b & 1 for b in range(LEVELS)]
    seps = []
    cpls = []
    for level in range(LEVELS):
        s = sep_share[0, level]
        c = coupling_share[0, level]
        for b in range(level + 1):
            s = scatter_sum(s, b, bits[b])
            c = scatter_sum(c, b, bits[b])
        s, c = gather_group(s, level), gather_group(c, level)
        seps.append(s.reshape(2 << level, 4, s.shape[1], SEP))
        cpls.append(c.reshape(2 << level, 4, c.shape[1], SEP))
    children = gather_group(child_update[0], 0).reshape(2, UPD, UPD)
    diag_parts = []
    below_parts = []
    current = None
    for level in range(LEVELS):
        if level == 0:
            first = (leaf >> 1) * 2
            child_ids = (first, first + 1)
            updates = (children,)
        else:
            own = leaf >> level
            child_ids = (own, own ^ 1)
            give = lax.dynamic_index_in_dim(current.reshape(2, 256, UPD), bits[0], 0, keepdims=False)
            near = swap(give, level)
            far = swap(near, 0)
            updates = (current, near, far)
        ids = jnp.concatenate(
            [lax.dynamic_index_in_dim(block_maps[level], i, 0, keepdims=False) for i in child_ids]
            + [jnp.stack([rid, bits[0]]).astype(jnp.int32)]
        )
        l_rows, r_rows, current = front(level, ids, seps[level], cpls[level], *updates)
        diag_parts.append(l_rows)
        below_parts.append(r_rows)
    return (jnp.stack(diag_parts)[None], jnp.stack(below_parts)[None], current[None])


def solution(mesh):
    return jax.shard_map(
        on_device,
        mesh=mesh,
        in_specs=(
            P("leaf", "rows", None),
            P(),
            P("leaf", None, "rows", None),
            P("leaf", None, "rows", None),
        ),
        out_specs=(
            P("leaf", None, "rows", None),
            P("leaf", None, "rows", None),
            P("leaf", "rows", None),
        ),
        check_vma=False,
    )
```

```python
import jax
import jax.numpy as jnp
from jax import lax
from jax.experimental import pallas as pl
from jax.experimental.pallas import tpu as pltpu
from jax.sharding import PartitionSpec as P

BLK = 128
SEP = 1024
UPD = 512
FRONT = SEP + UPD
LEVELS = 3
NSEP = SEP // BLK
PART = 8
f32 = jnp.float32
bf16 = jnp.bfloat16


def lane_b(x, c):
    return jnp.broadcast_to(x[:, c : c + 1], x.shape)


def sub_b(x, i):
    return jnp.broadcast_to(x[i : i + 1, :], x.shape)


def block_inverse(rows_a):
    groups = BLK // 8
    row = lax.broadcasted_iota(jnp.int32, (8, BLK), 0)
    lane = lax.broadcasted_iota(jnp.int32, (8, BLK), 1)
    M = list(rows_a)
    out = []
    for s in range(0, groups, PART):
        e = s + PART
        cols = [lane_b(M[s], 8 * s + j) for j in range(8)]
        zrows = []
        for b in range(s, e):
            c0 = 8 * b
            inside = (lane >= c0) & (lane < c0 + 8)
            coef = {g: [lane_b(M[g], c0 + k) for k in range(8)] for g in range(b + 1, e)}
            following = [lane_b(M[b + 1], c0 + 8 + j) for j in range(8)] if b + 1 < e else None
            X = jnp.where(inside, jnp.where(lane - c0 == row, 1.0, 0.0), M[b])
            rs = []
            zs = []
            ls = [[None] * 8 for _ in range(8)]
            pivot = sub_b(cols[0], 0)
            for k in range(8):
                r = lax.rsqrt(pivot)
                rs.append(r)
                if k < 7:
                    below = sub_b(cols[k], k + 1) * r
                    pivot = sub_b(cols[k + 1], k + 1) - below * below
                c = cols[k] * r
                for j in range(k + 1, 8):
                    ls[j][k] = sub_b(c, j)
                    cols[j] = cols[j] - c * ls[j][k]
                z = sub_b(X, k) * r
                zs.append(z)
                if k < 7:
                    X = X - jnp.where(row > k, c, 0.0) * z
            for g in range(b + 1, e):
                cg = coef[g]
                for k in range(8):
                    cg[k] = cg[k] * rs[k]
                    for i in range(k + 1, 8):
                        cg[i] = cg[i] - ls[i][k] * cg[k]
                m = jnp.where(inside, 0.0, M[g])
                for k in range(8):
                    m = m - cg[k] * zs[k]
                M[g] = m
                if g == b + 1:
                    for k in range(8):
                        for j in range(8):
                            following[j] = following[j] - cg[k] * sub_b(cg[k], j)
                    cols = following
            y = zs[0]
            for k in range(1, 8):
                y = jnp.where(row == k, zs[k], y)
            zrows.append(jnp.where((lane < c0 + 8) | (lane >= 8 * e), y, 0.0))
            out.append(jnp.where(lane < c0 + 8, y, 0.0))
        if e < groups:
            zh, zl = split(jnp.concatenate(zrows, axis=0))
            lhs = jnp.concatenate([zh, zh, zl], axis=0)[:, 8 * e :]
            rhs = jnp.concatenate([zh, zl, zh], axis=0)
            upd = lax.dot_general(lhs, rhs, (((0,), (0,)), ((), ())), preferred_element_type=f32)
            done = (lane >= 8 * s) & (lane < 8 * e)
            for g in range(e, groups):
                M[g] = jnp.where(done, 0.0, M[g]) - upd[8 * (g - e) : 8 * (g - e) + 8, :]
    return out


def split(x):
    hi = x.astype(bf16)
    return hi, (x - hi.astype(f32)).astype(bf16)


def nt(a, b):
    return lax.dot_general(a, b, (((1,), (1,)), ((), ())), preferred_element_type=f32)


def nt3(a_hi, a_lo, b_hi, b_lo):
    return nt(a_hi, b_hi) + (nt(a_hi, b_lo) + nt(a_lo, b_hi))


def blk(i):
    if isinstance(i, int):
        return pl.ds(i * BLK, BLK)
    return pl.ds(pl.multiple_of(i * BLK, BLK), BLK)


def front_body(level, refs):
    ids, mine, theirs = refs[:3]
    if level == 0:
        refs = refs[3:]
    else:
        own_in, near_in, far_in = refs[3:6]
        refs = refs[6:]
    l_out, r_out, u_out, F, C, Ub, Lh, Ll, Lf, T, D, E, Wh, Wl, sem = refs
    rid = ids[8]
    core = ids[9]
    wide = SEP // 2
    copies = []
    for src, half in ((mine, core), (theirs, 1 - core)):
        for r in range(4):
            for side in range(2):
                cols = pl.ds(side * wide, wide)
                sep_at = pl.multiple_of(r * 256 + half * BLK, BLK)
                cpl_at = pl.multiple_of(SEP + r * BLK + half * 64, 64)
                copies.append((src.at[r, pl.ds(side * BLK, BLK), :], F.at[pl.ds(sep_at, BLK), cols]))
                copies.append((src.at[r, pl.ds(256 + side * 64, 64), :], F.at[pl.ds(cpl_at, 64), cols]))
            if level == 0:
                copies.append((src.at[r, pl.ds(384, BLK), :], Ub.at[half, pl.ds(r * BLK, BLK), :]))
    if level > 0:
        copies.append((own_in, Ub.at[0]))
        copies.append((near_in, Ub.at[1, pl.ds(pl.multiple_of(core * 256, 256), 256), :]))
        copies.append((far_in, Ub.at[1, pl.ds(pl.multiple_of((1 - core) * 256, 256), 256), :]))
    copies = [pltpu.make_async_copy(s, t, sem.at[n]) for n, (s, t) in enumerate(copies)]
    for c in copies:
        c.start()
    C[...] = jnp.zeros_like(C)
    Lh[...] = jnp.zeros_like(Lh)
    Ll[...] = jnp.zeros_like(Ll)
    for c in copies:
        c.wait()

    def add_block(t, c):
        child = t // 16
        i = t // 4 % 4
        j = t % 4
        mi = ids[4 * child + i]
        mj = ids[4 * child + j]
        part = Ub[child, blk(i), blk(j)]

        @pl.when(mj < NSEP)
        def _():
            F[blk(mi), blk(mj)] += part

        @pl.when((mj >= NSEP) & (mi >= NSEP))
        def _():
            C[blk(jnp.maximum(mi - NSEP, 0)), blk(jnp.maximum(mj - NSEP, 0))] += part

        return c

    lax.fori_loop(0, 32, add_block, 0)
    D[...] = F[:BLK, :BLK]

    def panel(k, lo):
        th, tl = split(T[lo:, :])
        v = nt3(th, tl, Wh[...], Wl[...])
        Lf[lo:, blk(k)] = v
        h, l = split(v)
        Lh[lo:, blk(k)] = h
        Ll[lo:, blk(k)] = l

    def step(k, lo, depth):
        n = jnp.minimum(k + 1, NSEP - 1)
        panel(jnp.maximum(k - 1, 0), lo)
        T[lo:, :] = F[lo:, blk(k)] - nt3(
            Lh[lo:, :depth], Ll[lo:, :depth], Lh[blk(k), :depth], Ll[blk(k), :depth]
        )
        nh = Lh[blk(n), :depth]
        nl = Ll[blk(n), :depth]
        E[...] = F[blk(n), blk(n)] - nt3(nh, nl, nh, nl)
        W = jnp.concatenate(block_inverse([D[8 * g : 8 * g + 8, :] for g in range(BLK // 8)]), axis=0)
        wh, wl = split(W)
        Wh[...] = wh
        Wl[...] = wl
        th, tl = split(T[blk(n), :])
        h, l = split(nt3(th, tl, wh, wl))
        D[...] = E[...] - nt3(h, l, h, l)

    T[...] = jnp.zeros_like(T)
    Wh[...] = jnp.zeros_like(Wh)
    Wl[...] = jnp.zeros_like(Wl)
    lax.fori_loop(0, 4, lambda k, c: (step(k, 0, 512), c)[1], 0)
    lax.fori_loop(4, 8, lambda k, c: (step(k, 384, 1024), c)[1], 0)
    panel(7, 896)
    rh = Lh[SEP:, :]
    rl = Ll[SEP:, :]
    if level == LEVELS - 1:
        mine = pl.ds(pl.multiple_of(rid * BLK, BLK), BLK)
        mine_l = pl.ds(pl.multiple_of(SEP + rid * BLK, BLK), BLK)
        u_out[...] = C[mine, :] - nt3(Lh[mine_l, :], Ll[mine_l, :], rh, rl)
    else:
        u_out[...] = C[...] - nt3(rh, rl, rh, rl)
    rows = pl.ds(pl.multiple_of(rid * 256, 256), 256)
    ri = lax.broadcasted_iota(jnp.int32, (256, SEP), 0) + rid * 256
    ci = lax.broadcasted_iota(jnp.int32, (256, SEP), 1)
    l_out[...] = jnp.where(ri >= ci, Lf[rows, :], 0.0)
    r_out[...] = Lf[pl.ds(pl.multiple_of(SEP + rid * BLK, BLK), BLK), :]


def front(level, ids, mine, theirs, *updates):
    smem = pl.BlockSpec(memory_space=pltpu.SMEM)
    vmem = pl.BlockSpec(memory_space=pltpu.VMEM)
    hbm = pl.BlockSpec(memory_space=pl.ANY)
    last = level == LEVELS - 1
    copies = 40
    return pl.pallas_call(
        lambda *refs: front_body(level, refs),
        in_specs=[smem] + [hbm] * (2 + len(updates)),
        out_specs=[vmem] * 3,
        out_shape=[
            jax.ShapeDtypeStruct((256, SEP), f32),
            jax.ShapeDtypeStruct((BLK, SEP), f32),
            jax.ShapeDtypeStruct((BLK if last else UPD, UPD), f32),
        ],
        scratch_shapes=[
            pltpu.VMEM((FRONT, SEP), f32),
            pltpu.VMEM((UPD, UPD), f32),
            pltpu.VMEM((2, UPD, UPD), f32),
            pltpu.VMEM((FRONT, SEP), bf16),
            pltpu.VMEM((FRONT, SEP), bf16),
            pltpu.VMEM((FRONT, SEP), f32),
            pltpu.VMEM((FRONT, BLK), f32),
            pltpu.VMEM((BLK, BLK), f32),
            pltpu.VMEM((BLK, BLK), f32),
            pltpu.VMEM((BLK, BLK), bf16),
            pltpu.VMEM((BLK, BLK), bf16),
            pltpu.SemaphoreType.DMA((copies,)),
        ],
        compiler_params=pltpu.CompilerParams(vmem_limit_bytes=48 << 20),
        cost_estimate=pl.CostEstimate(flops=20_000_000_000, transcendentals=0, bytes_accessed=20_000_000),
        name=f"front{level}",
    )(ids, mine, theirs, *updates)


def swap(x, stride):
    return lax.ppermute(x, "leaf", [(i, i ^ 1 << stride) for i in range(lax.axis_size("leaf"))])


def pick(x, half, core):
    return lax.dynamic_slice_in_dim(x, core * half, half, x.ndim - 2)


def pack(sep, cpl, *rest):
    wide = SEP // 2
    return jnp.concatenate([sep[:, :wide], sep[:, wide:], cpl[:, :wide], cpl[:, wide:], *rest], axis=0)


def on_device(child_update, block_maps, sep_share, coupling_share):
    leaf = lax.axis_index("leaf")
    rid = lax.axis_index("rows")
    core = leaf & 1
    sep = sep_share[0]
    cpl = coupling_share[0]

    def pair_sum(levels):
        s = sep[levels]
        c = cpl[levels]
        return (
            pick(s, BLK, core) + swap(pick(s, BLK, 1 - core), 0),
            pick(c, 64, core) + swap(pick(c, 64, 1 - core), 0),
        )

    s0, c0 = pair_sum(slice(0, 1))
    first = lax.all_gather(pack(s0[0], c0[0], child_update[0]), "rows", axis=0, tiled=False)
    s12, c12 = pair_sum(slice(1, 3))
    later = jnp.stack([pack(s12[0], c12[0]), pack(s12[1], c12[1])])
    later = later + swap(later, 1)
    first, later = lax.optimization_barrier((first, later))
    mine = [first, lax.all_gather(later[0], "rows", axis=0, tiled=False), None]
    theirs = [swap(first, 0), None, None]
    p2 = later[1]
    far2 = swap(p2, 2)
    diag_parts = []
    below_parts = []
    current = None
    for level in range(LEVELS):
        own = leaf >> level
        updates = ()
        child_ids = (own, own ^ 1)
        if level == 0:
            child_ids = (own - core, own - core + 1)
        else:
            near = swap(lax.dynamic_slice_in_dim(current, core * 256, 256, 0), level)
            updates = (current, near, swap(near, 0))
            theirs[level] = swap(mine[level], 0)
        ids = jnp.concatenate(
            [lax.dynamic_index_in_dim(block_maps[level], i, 0, keepdims=False) for i in child_ids]
            + [jnp.stack([rid, core]).astype(jnp.int32)]
        )
        l_rows, r_rows, current = front(level, ids, mine[level], theirs[level], *updates)
        if level == 0:
            p2, mine[1], current = lax.optimization_barrier((p2, mine[1], current))
            mine[2] = lax.all_gather(p2 + far2, "rows", axis=0, tiled=False)
        elif level == 1:
            mine[2], current = lax.optimization_barrier((mine[2], current))
        diag_parts.append(l_rows)
        below_parts.append(r_rows)
    return (jnp.stack(diag_parts)[None], jnp.stack(below_parts)[None], current[None])


def solution(mesh):
    return jax.shard_map(
        on_device,
        mesh=mesh,
        in_specs=(
            P("leaf", "rows", None),
            P(),
            P("leaf", None, "rows", None),
            P("leaf", None, "rows", None),
        ),
        out_specs=(
            P("leaf", None, "rows", None),
            P("leaf", None, "rows", None),
            P("leaf", "rows", None),
        ),
        check_vma=False,
    )
```

```python
import jax
import jax.numpy as jnp
from jax import lax
from jax.experimental import pallas as pl
from jax.experimental.pallas import tpu as pltpu
from jax.sharding import PartitionSpec as P

BLK = 128
SEP = 1024
UPD = 512
FRONT = SEP + UPD
LEVELS = 3
NSEP = SEP // BLK
NUPD = UPD // BLK
PART = 8
HALVES = (((0, 0), (1, 0), (1, 1), (2, 0), (2, 1)), ((2, 2), (3, 0), (3, 1), (3, 2), (3, 3)))
f32 = jnp.float32
bf16 = jnp.bfloat16


def lane_b(x, c):
    return jnp.broadcast_to(x[:, c : c + 1], x.shape)


def sub_b(x, i):
    return jnp.broadcast_to(x[i : i + 1, :], x.shape)


def block_inverse(rows_a):
    groups = BLK // 8
    row = lax.broadcasted_iota(jnp.int32, (8, BLK), 0)
    lane = lax.broadcasted_iota(jnp.int32, (8, BLK), 1)
    M = list(rows_a)
    out = []
    for s in range(0, groups, PART):
        e = s + PART
        cols = [lane_b(M[s], 8 * s + j) for j in range(8)]
        zrows = []
        for b in range(s, e):
            c0 = 8 * b
            inside = (lane >= c0) & (lane < c0 + 8)
            coef = {g: [lane_b(M[g], c0 + k) for k in range(8)] for g in range(b + 1, e)}
            following = [lane_b(M[b + 1], c0 + 8 + j) for j in range(8)] if b + 1 < e else None
            X = jnp.where(inside, jnp.where(lane - c0 == row, 1.0, 0.0), M[b])
            rs = []
            zs = []
            ls = [[None] * 8 for _ in range(8)]
            pivot = sub_b(cols[0], 0)
            for k in range(8):
                r = lax.rsqrt(pivot)
                rs.append(r)
                if k < 7:
                    below = sub_b(cols[k], k + 1) * r
                    pivot = sub_b(cols[k + 1], k + 1) - below * below
                c = cols[k] * r
                for j in range(k + 1, 8):
                    ls[j][k] = sub_b(c, j)
                    cols[j] = cols[j] - c * ls[j][k]
                z = sub_b(X, k) * r
                zs.append(z)
                if k < 7:
                    X = X - jnp.where(row > k, c, 0.0) * z
            for g in range(b + 1, e):
                cg = coef[g]
                for k in range(8):
                    cg[k] = cg[k] * rs[k]
                    for i in range(k + 1, 8):
                        cg[i] = cg[i] - ls[i][k] * cg[k]
                m = jnp.where(inside, 0.0, M[g])
                for k in range(8):
                    m = m - cg[k] * zs[k]
                M[g] = m
                if g == b + 1:
                    for k in range(8):
                        for j in range(8):
                            following[j] = following[j] - cg[k] * sub_b(cg[k], j)
                    cols = following
            y = zs[0]
            for k in range(1, 8):
                y = jnp.where(row == k, zs[k], y)
            zrows.append(jnp.where((lane < c0 + 8) | (lane >= 8 * e), y, 0.0))
            out.append(jnp.where(lane < c0 + 8, y, 0.0))
        if e < groups:
            zh, zl = split(jnp.concatenate(zrows, axis=0))
            lhs = jnp.concatenate([zh, zh, zl], axis=0)[:, 8 * e :]
            rhs = jnp.concatenate([zh, zl, zh], axis=0)
            upd = lax.dot_general(lhs, rhs, (((0,), (0,)), ((), ())), preferred_element_type=f32)
            done = (lane >= 8 * s) & (lane < 8 * e)
            for g in range(e, groups):
                M[g] = jnp.where(done, 0.0, M[g]) - upd[8 * (g - e) : 8 * (g - e) + 8, :]
    return out


def split(x):
    hi = x.astype(bf16)
    return hi, (x - hi.astype(f32)).astype(bf16)


def nt(a, b):
    return lax.dot_general(a, b, (((1,), (1,)), ((), ())), preferred_element_type=f32)


def nt3(a_hi, a_lo, b_hi, b_lo):
    return nt(a_hi, b_hi) + (nt(a_hi, b_lo) + nt(a_lo, b_hi))


def blk(i):
    if isinstance(i, int):
        return pl.ds(i * BLK, BLK)
    return pl.ds(pl.multiple_of(i * BLK, BLK), BLK)


def front_body(level, refs):
    last = level == LEVELS - 1
    ids = refs[0]
    if level == 0:
        pieces, refs = refs[1:11], refs[11:]
    else:
        mine, theirs, own_in, near_in, far_in = refs[1:6]
        refs = refs[8:]
    l_all, r_all, u_out = refs[:3]
    refs = refs[3:]
    if not last:
        give_out, refs = refs[0], refs[1:]
    F, G, C, UG, Ub, Lh, Ll, Lf, T, D, E, Wh, Wl, Lo, Ro, sem = refs
    rid = ids[8]
    core = ids[9]
    copies = []

    def take(src, r, half, lo, hi):
        i = 2 * r + half
        copies.append((src.at[:, pl.ds(0, 640)], G.at[i, pl.ds(lo, hi - lo), :]))
        at = pl.multiple_of(SEP + r * BLK + half * 64, 64)
        for side in range(2):
            if lo <= side * 64 < hi:
                copies.append(
                    (src.at[pl.ds(side * 64 - lo, 64), pl.ds(640, 512)], F.at[pl.ds(at, 64), pl.ds(side * 512, 512)])
                )
        if level == 0:
            copies.append((src.at[:, pl.ds(1152, 384)], UG.at[half, r, pl.ds(lo, hi - lo), :]))

    if level == 0:
        for n, half in ((0, core), (5, 1 - core)):
            take(pieces[n], rid, half, 0, BLK)
            take(pieces[n + 1], (rid + 3) % 4, half, 0, BLK)
            take(pieces[n + 2], (rid + 1) % 4, half, 0, BLK)
            take(pieces[n + 3], (rid + 2) % 4, half, 0, 64)
            take(pieces[n + 4], (rid + 2) % 4, half, 64, BLK)
    else:
        for src, half in ((mine, core), (theirs, 1 - core)):
            for r in range(4):
                take(src.at[r], r, half, 0, BLK)
        copies.append((own_in, UG.at[0]))
        copies.append((near_in, UG.at[1, core]))
        copies.append((far_in, UG.at[1, 1 - core]))
    copies = [pltpu.make_async_copy(s, t, sem.at[n]) for n, (s, t) in enumerate(copies)]
    for c in copies:
        c.start()
    C[...] = jnp.zeros_like(C)
    Lh[...] = jnp.zeros_like(Lh)
    Ll[...] = jnp.zeros_like(Ll)
    T[...] = jnp.zeros_like(T)
    Wh[...] = jnp.zeros_like(Wh)
    Wl[...] = jnp.zeros_like(Wl)
    for c in copies:
        c.wait()
    for i in range(NSEP):
        for d in range(5):
            j = (i - d) % NSEP
            part = G[i, :, BLK * d : BLK * d + BLK]
            if i >= j:
                F[blk(i), blk(j)] = part
            elif d < 4:
                F[blk(j), blk(i)] = part.T
    for child in range(2):
        parts = {}
        if level == 0:
            for r in range(NUPD):
                for d in range(3):
                    if d < 2 or r >= 2:
                        parts[r, (r - d) % NUPD] = UG[child, r, :, BLK * d : BLK * d + BLK]
        else:
            for half in range(2):
                for n, ij in enumerate(HALVES[half]):
                    parts[ij] = UG[child, half, :, BLK * n : BLK * n + BLK]
        for (i, j), part in parts.items():
            Ub[child, blk(i), blk(j)] = part
            if i != j:
                Ub[child, blk(j), blk(i)] = part.T

    def add_block(t, c):
        child = t // 16
        i = t // 4 % 4
        j = t % 4
        mi = ids[4 * child + i]
        mj = ids[4 * child + j]

        @pl.when((mj < NSEP) & (mi >= mj))
        def _():
            F[blk(mi), blk(mj)] += Ub[child, blk(i), blk(j)]

        @pl.when((mj >= NSEP) & (mi >= NSEP))
        def _():
            C[blk(jnp.maximum(mi - NSEP, 0)), blk(jnp.maximum(mj - NSEP, 0))] += Ub[child, blk(i), blk(j)]

        return c

    lax.fori_loop(0, 32, add_block, 0)
    D[...] = F[:BLK, :BLK]

    def panel(k, lo):
        th, tl = split(T[lo:, :])
        v = nt3(th, tl, Wh[...], Wl[...])
        Lf[lo:, blk(k)] = v
        h, l = split(v)
        Lh[lo:, blk(k)] = h
        Ll[lo:, blk(k)] = l

    def step(k, lo, depth):
        n = jnp.minimum(k + 1, NSEP - 1)
        panel(jnp.maximum(k - 1, 0), lo)
        T[lo:, :] = F[lo:, blk(k)] - nt3(
            Lh[lo:, :depth], Ll[lo:, :depth], Lh[blk(k), :depth], Ll[blk(k), :depth]
        )
        nh = Lh[blk(n), :depth]
        nl = Ll[blk(n), :depth]
        E[...] = F[blk(n), blk(n)] - nt3(nh, nl, nh, nl)
        W = jnp.concatenate(block_inverse([D[8 * g : 8 * g + 8, :] for g in range(BLK // 8)]), axis=0)
        wh, wl = split(W)
        Wh[...] = wh
        Wl[...] = wl
        th, tl = split(T[blk(n), :])
        h, l = split(nt3(th, tl, wh, wl))
        D[...] = E[...] - nt3(h, l, h, l)

    lax.fori_loop(0, 4, lambda k, c: (step(k, 0, 512), c)[1], 0)
    lax.fori_loop(4, 8, lambda k, c: (step(k, 384, 1024), c)[1], 0)
    panel(7, 896)
    rows = pl.ds(pl.multiple_of(rid * 256, 256), 256)
    ri = lax.broadcasted_iota(jnp.int32, (256, SEP), 0) + rid * 256
    ci = lax.broadcasted_iota(jnp.int32, (256, SEP), 1)
    Lo[...] = jnp.where(ri >= ci, Lf[rows, :], 0.0)
    Ro[...] = Lf[pl.ds(pl.multiple_of(SEP + rid * BLK, BLK), BLK), :]
    writes = [
        pltpu.make_async_copy(Lo, l_all.at[level], sem.at[0]),
        pltpu.make_async_copy(Ro, r_all.at[level], sem.at[1]),
    ]
    for c in writes:
        c.start()
    if last:
        mine_u = pl.ds(pl.multiple_of(rid * BLK, BLK), BLK)
        mine_l = pl.ds(pl.multiple_of(SEP + rid * BLK, BLK), BLK)
        u_out[...] = C[mine_u, :] - nt3(Lh[mine_l, :], Ll[mine_l, :], Lh[SEP:, :], Ll[SEP:, :])
    else:
        place = {ij: (half, n) for half in range(2) for n, ij in enumerate(HALVES[half])}
        for i in range(NUPD):
            left = pl.ds(SEP + i * BLK, BLK)
            upto = pl.ds(SEP, BLK * (i + 1))
            new = C[blk(i), : BLK * (i + 1)] - nt3(Lh[left, :], Ll[left, :], Lh[upto, :], Ll[upto, :])
            for j in range(i + 1):
                half, n = place[i, j]
                u_out[half, :, BLK * n : BLK * n + BLK] = new[:, BLK * j : BLK * j + BLK]
        give_out[...] = u_out[core]
    for c in writes:
        c.wait()


def front(level, ids, *inputs):
    smem = pl.BlockSpec(memory_space=pltpu.SMEM)
    vmem = pl.BlockSpec(memory_space=pltpu.VMEM)
    hbm = pl.BlockSpec(memory_space=pl.ANY)
    last = level == LEVELS - 1
    update = [(BLK, UPD)] if last else [(2, BLK, 640), (BLK, 640)]
    shapes = [(LEVELS, 256, SEP), (LEVELS, BLK, SEP)] + update
    return pl.pallas_call(
        lambda *refs: front_body(level, refs),
        in_specs=[smem] + [hbm] * len(inputs),
        out_specs=[hbm] * 2 + [vmem] * len(update),
        out_shape=[jax.ShapeDtypeStruct(s, f32) for s in shapes],
        input_output_aliases={} if level == 0 else {6: 0, 7: 1},
        scratch_shapes=[
            pltpu.VMEM((FRONT, SEP), f32),
            pltpu.VMEM((NSEP, BLK, 640), f32),
            pltpu.VMEM((UPD, UPD), f32),
            pltpu.VMEM((2, 4, BLK, 384) if level == 0 else (2, 2, BLK, 640), f32),
            pltpu.VMEM((2, UPD, UPD), f32),
            pltpu.VMEM((FRONT, SEP), bf16),
            pltpu.VMEM((FRONT, SEP), bf16),
            pltpu.VMEM((FRONT, SEP), f32),
            pltpu.VMEM((FRONT, BLK), f32),
            pltpu.VMEM((BLK, BLK), f32),
            pltpu.VMEM((BLK, BLK), f32),
            pltpu.VMEM((BLK, BLK), bf16),
            pltpu.VMEM((BLK, BLK), bf16),
            pltpu.VMEM((256, SEP), f32),
            pltpu.VMEM((BLK, SEP), f32),
            pltpu.SemaphoreType.DMA((40,)),
        ],
        compiler_params=pltpu.CompilerParams(vmem_limit_bytes=48 << 20),
        cost_estimate=pl.CostEstimate(flops=20_000_000_000, transcendentals=0, bytes_accessed=20_000_000),
        name=f"front{level}",
    )(ids, *inputs)


def pack_body(with_child, refs):
    ids, sep, cpl = refs[:3]
    refs = refs[3:]
    if with_child:
        child, refs = refs[0], refs[1:]
    give, keep = refs[:2]
    rid = ids[0]
    core = ids[1]
    for out, half in ((give, 1 - core), (keep, core)):
        i = 2 * rid + half
        rows = pl.ds(pl.multiple_of(half * BLK, BLK), BLK)
        for d in range(5):
            out[0, :, BLK * d : BLK * d + BLK] = sep[0, rows, blk((i + NSEP - d) % NSEP)]
        for side in range(2):
            at = pl.ds(pl.multiple_of(half * 64, 64), 64)
            out[0, 64 * side : 64 * side + 64, 640:] = cpl[0, at, 512 * side : 512 * side + 512]
    if with_child:
        for d in range(3):
            refs[2][:, BLK * d : BLK * d + BLK] = child[:, blk((rid + NUPD - d) % NUPD)]


def pack_shares(first, count, ids, sep, cpl, *child):
    return pl.pallas_call(
        lambda *refs: pack_body(len(child) > 0, refs),
        grid=(count,),
        in_specs=[
            pl.BlockSpec(memory_space=pltpu.SMEM),
            pl.BlockSpec((1, 256, SEP), lambda n: (first + n, 0, 0)),
            pl.BlockSpec((1, BLK, SEP), lambda n: (first + n, 0, 0)),
        ]
        + [pl.BlockSpec((BLK, UPD), lambda n: (0, 0))] * len(child),
        out_specs=[pl.BlockSpec((1, BLK, 1152), lambda n: (n, 0, 0))] * 2
        + [pl.BlockSpec((BLK, 384), lambda n: (0, 0))] * len(child),
        out_shape=[jax.ShapeDtypeStruct((count, BLK, 1152), f32)] * 2
        + [jax.ShapeDtypeStruct((BLK, 384), f32)] * len(child),
        name=f"pack{first}",
    )(ids, sep, cpl, *child)


def swap(x, stride):
    return lax.ppermute(x, "leaf", [(i, i ^ 1 << stride) for i in range(lax.axis_size("leaf"))])


def shift(x, by):
    size = lax.axis_size("rows")
    return lax.ppermute(x, "rows", [(i, (i + by) % size) for i in range(size)])


def turn(x, by):
    return lax.ppermute(x, "leaf", [(i, i ^ (by << 1)) for i in range(lax.axis_size("leaf"))])


def on_device(child_update, block_maps, sep_share, coupling_share):
    leaf = lax.axis_index("leaf")
    rid = lax.axis_index("rows")
    core = leaf & 1
    sep = sep_share[0]
    cpl = coupling_share[0]
    where = jnp.stack([rid, core]).astype(jnp.int32)

    give, keep, child = pack_shares(0, 1, where, sep, cpl, child_update[0])
    own = jnp.concatenate([keep[0] + swap(give[0], 0), child], axis=1)
    left = shift(own, 1)
    right = shift(own, -1)
    opp = [shift(left[:64], 1), shift(right[64:], -1)]
    near = [own, left, right] + opp
    far = [swap(x, 0) for x in near]

    give, keep = pack_shares(1, 2, where, sep, cpl)
    later = keep + swap(give, 0)
    p1 = later[0] + swap(later[0], 1)
    opp[0], opp[1], p1, later = lax.optimization_barrier((opp[0], opp[1], p1, later))
    near[3:] = opp
    far[3:] = [swap(x, 0) for x in opp]
    mine = [None, lax.all_gather(p1, "rows", axis=0, tiled=False), None]
    p2 = later[1]
    others = [turn(p2, by) for by in (1, 2, 3)]

    l_all = r_all = current = give = None
    for level in range(LEVELS):
        me = leaf >> level
        child_ids = (me - core, me - core + 1) if level == 0 else (me, me ^ 1)
        ids = jnp.concatenate(
            [lax.dynamic_index_in_dim(block_maps[level], i, 0, keepdims=False) for i in child_ids] + [where]
        )
        if level == 0:
            l_all, r_all, current, give = front(0, ids, *near, *far)
            p2, mine[1], current, give = lax.optimization_barrier((p2, mine[1], current, give))
            mine[2] = lax.all_gather(p2 + others[0] + others[1] + others[2], "rows", axis=0, tiled=False)
            continue
        got = swap(give, level)
        inputs = (mine[level], swap(mine[level], 0), current, got, swap(got, 0), l_all, r_all)
        if level == 1:
            l_all, r_all, current, give = front(1, ids, *inputs)
            mine[2], current, give = lax.optimization_barrier((mine[2], current, give))
        else:
            l_all, r_all, top = front(2, ids, *inputs)
    return l_all[None], r_all[None], top[None]


def solution(mesh):
    return jax.shard_map(
        on_device,
        mesh=mesh,
        in_specs=(
            P("leaf", "rows", None),
            P(),
            P("leaf", None, "rows", None),
            P("leaf", None, "rows", None),
        ),
        out_specs=(
            P("leaf", None, "rows", None),
            P("leaf", None, "rows", None),
            P("leaf", "rows", None),
        ),
        check_vma=False,
    )
```

```python
import jax
import jax.numpy as jnp
from jax import lax
from jax.experimental import pallas as pl
from jax.experimental.pallas import tpu as pltpu
from jax.sharding import PartitionSpec as P

BLK = 128
SEP = 1024
UPD = 512
FRONT = SEP + UPD
LEVELS = 3
NSEP = SEP // BLK
NUPD = UPD // BLK
PART = 8
PAIR = 2 * BLK
CHUNK = 4
HALVES = (((0, 0), (1, 0), (1, 1), (2, 0), (2, 1)), ((2, 2), (3, 0), (3, 1), (3, 2), (3, 3)))
f32 = jnp.float32
bf16 = jnp.bfloat16


def lane_b(x, c):
    return jnp.broadcast_to(x[:, c : c + 1], x.shape)


def sub_b(x, i):
    return jnp.broadcast_to(x[i : i + 1, :], x.shape)


def block_inverse(rows_a):
    groups = BLK // 8
    row = lax.broadcasted_iota(jnp.int32, (8, BLK), 0)
    lane = lax.broadcasted_iota(jnp.int32, (8, BLK), 1)
    M = list(rows_a)
    out = []
    for s in range(0, groups, PART):
        e = s + PART
        cols = [lane_b(M[s], 8 * s + j) for j in range(8)]
        zrows = []
        for b in range(s, e):
            c0 = 8 * b
            inside = (lane >= c0) & (lane < c0 + 8)
            coef = {g: [lane_b(M[g], c0 + k) for k in range(8)] for g in range(b + 1, e)}
            following = [lane_b(M[b + 1], c0 + 8 + j) for j in range(8)] if b + 1 < e else None
            X = jnp.where(inside, jnp.where(lane - c0 == row, 1.0, 0.0), M[b])
            rs = []
            zs = []
            ls = [[None] * 8 for _ in range(8)]
            pivot = sub_b(cols[0], 0)
            for k in range(8):
                r = lax.rsqrt(pivot)
                rs.append(r)
                if k < 7:
                    below = sub_b(cols[k], k + 1) * r
                    pivot = sub_b(cols[k + 1], k + 1) - below * below
                c = cols[k] * r
                for j in range(k + 1, 8):
                    ls[j][k] = sub_b(c, j)
                    cols[j] = cols[j] - c * ls[j][k]
                z = sub_b(X, k) * r
                zs.append(z)
                if k < 7:
                    X = X - jnp.where(row > k, c, 0.0) * z
            for g in range(b + 1, e):
                cg = coef[g]
                for k in range(8):
                    cg[k] = cg[k] * rs[k]
                    for i in range(k + 1, 8):
                        cg[i] = cg[i] - ls[i][k] * cg[k]
                m = jnp.where(inside, 0.0, M[g])
                for k in range(8):
                    m = m - cg[k] * zs[k]
                M[g] = m
                if g == b + 1:
                    for k in range(8):
                        for j in range(8):
                            following[j] = following[j] - cg[k] * sub_b(cg[k], j)
                    cols = following
            y = zs[0]
            for k in range(1, 8):
                y = jnp.where(row == k, zs[k], y)
            zrows.append(jnp.where((lane < c0 + 8) | (lane >= 8 * e), y, 0.0))
            out.append(jnp.where(lane < c0 + 8, y, 0.0))
        if e < groups:
            zh, zl = split(jnp.concatenate(zrows, axis=0))
            lhs = jnp.concatenate([zh, zh, zl], axis=0)[:, 8 * e :]
            rhs = jnp.concatenate([zh, zl, zh], axis=0)
            upd = lax.dot_general(lhs, rhs, (((0,), (0,)), ((), ())), preferred_element_type=f32)
            done = (lane >= 8 * s) & (lane < 8 * e)
            for g in range(e, groups):
                M[g] = jnp.where(done, 0.0, M[g]) - upd[8 * (g - e) : 8 * (g - e) + 8, :]
    return out


def split(x):
    hi = x.astype(bf16)
    return hi, (x - hi.astype(f32)).astype(bf16)


def nt(a, b):
    return lax.dot_general(a, b, (((1,), (1,)), ((), ())), preferred_element_type=f32)


def stack_split(x):
    hi, lo = split(x)
    rows = x.shape[0] // BLK
    parts = []
    for i in range(rows):
        parts += [hi[i * BLK : (i + 1) * BLK], lo[i * BLK : (i + 1) * BLK]]
    return jnp.concatenate(parts, axis=0)


def nt4(a, b):
    p = nt(a, b)
    rows = []
    for i in range(a.shape[0] // PAIR):
        cols = []
        for j in range(b.shape[0] // PAIR):
            q = p[i * PAIR : (i + 1) * PAIR, j * PAIR : (j + 1) * PAIR]
            cols.append(q[:BLK, :BLK] + (q[:BLK, BLK:] + q[BLK:, :BLK]) + q[BLK:, BLK:])
        rows.append(cols[0] if len(cols) == 1 else jnp.concatenate(cols, axis=1))
    return rows[0] if len(rows) == 1 else jnp.concatenate(rows, axis=0)


def blk(i):
    if isinstance(i, int):
        return pl.ds(i * BLK, BLK)
    return pl.ds(pl.multiple_of(i * BLK, BLK), BLK)


def two(i, n=1):
    if isinstance(i, int):
        return pl.ds(i * PAIR, n * PAIR)
    return pl.ds(pl.multiple_of(i * PAIR, PAIR), n * PAIR)


def chunks(lo):
    first = lo // BLK
    for i in range(first, FRONT // BLK, CHUNK):
        yield i, min(CHUNK, FRONT // BLK - i)


def front_body(level, refs):
    last = level == LEVELS - 1
    ids = refs[0]
    if level == 0:
        pieces, refs = refs[1:11], refs[11:]
    else:
        mine, theirs, own_in, near_in, far_in = refs[1:6]
        refs = refs[8:]
    l_all, r_all, u_out = refs[:3]
    refs = refs[3:]
    if not last:
        give_out, refs = refs[0], refs[1:]
    F, G, C, UG, Ub, LL, Lf, T, D, E, WW, Lo, Ro, Uo, sem = refs
    rid = ids[8]
    core = ids[9]
    copies = []

    def take(src, r, half, lo, hi):
        i = 2 * r + half
        copies.append((src.at[:, pl.ds(0, 640)], G.at[i, pl.ds(lo, hi - lo), :]))
        at = pl.multiple_of(SEP + r * BLK + half * 64, 64)
        for side in range(2):
            if lo <= side * 64 < hi:
                copies.append(
                    (src.at[pl.ds(side * 64 - lo, 64), pl.ds(640, 512)], F.at[pl.ds(at, 64), pl.ds(side * 512, 512)])
                )
        if level == 0:
            copies.append((src.at[:, pl.ds(1152, 384)], UG.at[half, r, pl.ds(lo, hi - lo), :]))

    if level == 0:
        for n, half in ((0, core), (5, 1 - core)):
            take(pieces[n], rid, half, 0, BLK)
            take(pieces[n + 1], (rid + 3) % 4, half, 0, BLK)
            take(pieces[n + 2], (rid + 1) % 4, half, 0, BLK)
            take(pieces[n + 3], (rid + 2) % 4, half, 0, 64)
            take(pieces[n + 4], (rid + 2) % 4, half, 64, BLK)
    else:
        for src, half in ((mine, core), (theirs, 1 - core)):
            for r in range(4):
                take(src.at[r], r, half, 0, BLK)
        copies.append((own_in, UG.at[0]))
        copies.append((near_in, UG.at[1, core]))
        copies.append((far_in, UG.at[1, 1 - core]))
    copies = [pltpu.make_async_copy(s, t, sem.at[n]) for n, (s, t) in enumerate(copies)]
    for c in copies:
        c.start()
    C[...] = jnp.zeros_like(C)
    LL[...] = jnp.zeros_like(LL)
    T[...] = jnp.zeros_like(T)
    WW[...] = jnp.zeros_like(WW)
    for c in copies:
        c.wait()
    for i in range(NSEP):
        for d in range(5):
            j = (i - d) % NSEP
            part = G[i, :, BLK * d : BLK * d + BLK]
            if i >= j:
                F[blk(i), blk(j)] = part
            elif d < 4:
                F[blk(j), blk(i)] = part.T
    for child in range(2):
        parts = {}
        if level == 0:
            for r in range(NUPD):
                for d in range(3):
                    if d < 2 or r >= 2:
                        parts[r, (r - d) % NUPD] = UG[child, r, :, BLK * d : BLK * d + BLK]
        else:
            for half in range(2):
                for n, ij in enumerate(HALVES[half]):
                    parts[ij] = UG[child, half, :, BLK * n : BLK * n + BLK]
        for (i, j), part in parts.items():
            Ub[child, blk(i), blk(j)] = part
            if i != j:
                Ub[child, blk(j), blk(i)] = part.T

    def add_block(t, c):
        child = t // 10
        p = t % 10
        i = (p >= 1).astype(jnp.int32) + (p >= 3).astype(jnp.int32) + (p >= 6).astype(jnp.int32)
        j = p - i * (i + 1) // 2
        mi = ids[4 * child + i]
        mj = ids[4 * child + j]
        si = jnp.where(mi >= mj, i, j)
        sj = i + j - si
        hi = jnp.maximum(mi, mj)
        lo = jnp.minimum(mi, mj)

        @pl.when(lo < NSEP)
        def _():
            F[blk(hi), blk(lo)] += Ub[child, blk(si), blk(sj)]

        @pl.when(lo >= NSEP)
        def _():
            h = jnp.maximum(hi - NSEP, 0)
            l = jnp.maximum(lo - NSEP, 0)
            C[blk(h), blk(l)] += Ub[child, blk(si), blk(sj)]
            if last:

                @pl.when(i > j)
                def _():
                    C[blk(l), blk(h)] += Ub[child, blk(sj), blk(si)]

        return c

    lax.fori_loop(0, 20, add_block, 0)
    D[...] = F[:BLK, :BLK]

    def panel(k, lo):
        for i, n in chunks(lo):
            rows = pl.ds(i * BLK, n * BLK)
            v = nt4(stack_split(T[rows, :]), WW[...])
            Lf[rows, blk(k)] = v
            LL[two(i, n), blk(k)] = stack_split(v)

    def step(k, lo, depth):
        nxt = jnp.minimum(k + 1, NSEP - 1)
        panel(jnp.maximum(k - 1, 0), lo)
        for i, n in chunks(lo):
            rows = pl.ds(i * BLK, n * BLK)
            T[rows, :] = F[rows, blk(k)] - nt4(LL[two(i, n), :depth], LL[two(k), :depth])
        near = LL[two(nxt), :depth]
        E[...] = F[blk(nxt), blk(nxt)] - nt4(near, near)
        W = jnp.concatenate(block_inverse([D[8 * g : 8 * g + 8, :] for g in range(BLK // 8)]), axis=0)
        WW[...] = stack_split(W)
        l = stack_split(nt4(stack_split(T[blk(nxt), :]), WW[...]))
        D[...] = E[...] - nt4(l, l)

    lax.fori_loop(0, 4, lambda k, c: (step(k, 0, 384), c)[1], 0)
    lax.fori_loop(4, 8, lambda k, c: (step(k, 384, 896), c)[1], 0)
    panel(7, 896)
    rows = pl.ds(pl.multiple_of(rid * 256, 256), 256)
    ri = lax.broadcasted_iota(jnp.int32, (256, SEP), 0) + rid * 256
    ci = lax.broadcasted_iota(jnp.int32, (256, SEP), 1)
    Lo[...] = jnp.where(ri >= ci, Lf[rows, :], 0.0)
    Ro[...] = Lf[pl.ds(pl.multiple_of(SEP + rid * BLK, BLK), BLK), :]
    writes = [
        pltpu.make_async_copy(Lo, l_all.at[level], sem.at[0]),
        pltpu.make_async_copy(Ro, r_all.at[level], sem.at[1]),
    ]
    for c in writes:
        c.start()
    if last:
        mine_u = pl.ds(pl.multiple_of(rid * BLK, BLK), BLK)
        u_out[...] = C[mine_u, :] - nt4(LL[two(NSEP + rid), :], LL[two(NSEP, NUPD), :])
    else:
        place = {ij: (half, n) for half in range(2) for n, ij in enumerate(HALVES[half])}
        for i in range(NUPD):
            new = C[blk(i), : BLK * (i + 1)] - nt4(LL[two(NSEP + i), :], LL[two(NSEP, i + 1), :])
            for j in range(i + 1):
                half, n = place[i, j]
                Uo[half, :, BLK * n : BLK * n + BLK] = new[:, BLK * j : BLK * j + BLK]
        writes += [
            pltpu.make_async_copy(Uo, u_out, sem.at[2]),
            pltpu.make_async_copy(Uo.at[core], give_out, sem.at[3]),
        ]
        for c in writes[2:]:
            c.start()
    for c in writes:
        c.wait()


def front(level, ids, *inputs):
    smem = pl.BlockSpec(memory_space=pltpu.SMEM)
    vmem = pl.BlockSpec(memory_space=pltpu.VMEM)
    hbm = pl.BlockSpec(memory_space=pltpu.HBM)
    last = level == LEVELS - 1
    update = [(BLK, UPD)] if last else [(2, BLK, 640), (BLK, 640)]
    shapes = [(LEVELS, 256, SEP), (LEVELS, BLK, SEP)] + update
    return pl.pallas_call(
        lambda *refs: front_body(level, refs),
        in_specs=[smem] + [hbm] * len(inputs),
        out_specs=[hbm] * 2 + ([vmem] if last else [hbm] * 2),
        out_shape=[jax.ShapeDtypeStruct(s, f32) for s in shapes],
        input_output_aliases={} if level == 0 else {6: 0, 7: 1},
        scratch_shapes=[
            pltpu.VMEM((FRONT, SEP), f32),
            pltpu.VMEM((NSEP, BLK, 640), f32),
            pltpu.VMEM((UPD, UPD), f32),
            pltpu.VMEM((2, 4, BLK, 384) if level == 0 else (2, 2, BLK, 640), f32),
            pltpu.VMEM((2, UPD, UPD), f32),
            pltpu.VMEM((2 * FRONT, SEP), bf16),
            pltpu.VMEM((FRONT, SEP), f32),
            pltpu.VMEM((FRONT, BLK), f32),
            pltpu.VMEM((BLK, BLK), f32),
            pltpu.VMEM((BLK, BLK), f32),
            pltpu.VMEM((PAIR, BLK), bf16),
            pltpu.VMEM((256, SEP), f32),
            pltpu.VMEM((BLK, SEP), f32),
            pltpu.VMEM((2, BLK, 640), f32),
            pltpu.SemaphoreType.DMA((40,)),
        ],
        compiler_params=pltpu.CompilerParams(vmem_limit_bytes=60 << 20),
        cost_estimate=pl.CostEstimate(flops=20_000_000_000, transcendentals=0, bytes_accessed=20_000_000),
        name=f"front{level}",
    )(ids, *inputs)


def pack_body(with_child, refs):
    ids, sep, cpl = refs[:3]
    refs = refs[3:]
    if with_child:
        child, refs = refs[0], refs[1:]
    give, keep = refs[:2]
    rid = ids[0]
    core = ids[1]
    for out, half in ((give, 1 - core), (keep, core)):
        i = 2 * rid + half
        rows = pl.ds(pl.multiple_of(half * BLK, BLK), BLK)
        for d in range(5):
            out[:, BLK * d : BLK * d + BLK] = sep[0, rows, blk((i + NSEP - d) % NSEP)]
        for side in range(2):
            at = pl.ds(pl.multiple_of(half * 64, 64), 64)
            out[64 * side : 64 * side + 64, 640:] = cpl[0, at, 512 * side : 512 * side + 512]
    if with_child:
        for d in range(3):
            refs[2][:, BLK * d : BLK * d + BLK] = child[:, blk((rid + NUPD - d) % NUPD)]


def pack_shares(level, ids, sep, cpl, *child):
    return pl.pallas_call(
        lambda *refs: pack_body(len(child) > 0, refs),
        grid=(1,),
        in_specs=[
            pl.BlockSpec(memory_space=pltpu.SMEM),
            pl.BlockSpec((1, 256, SEP), lambda n: (level, 0, 0)),
            pl.BlockSpec((1, BLK, SEP), lambda n: (level, 0, 0)),
        ]
        + [pl.BlockSpec((BLK, UPD), lambda n: (0, 0))] * len(child),
        out_specs=[pl.BlockSpec((BLK, 1152), lambda n: (0, 0))] * 2
        + [pl.BlockSpec((BLK, 384), lambda n: (0, 0))] * len(child),
        out_shape=[jax.ShapeDtypeStruct((BLK, 1152), f32)] * 2
        + [jax.ShapeDtypeStruct((BLK, 384), f32)] * len(child),
        name=f"pack{level}",
    )(ids, sep, cpl, *child)


def swap(x, stride):
    return lax.ppermute(x, "leaf", [(i, i ^ 1 << stride) for i in range(lax.axis_size("leaf"))])


def shift(x, by):
    size = lax.axis_size("rows")
    return lax.ppermute(x, "rows", [(i, (i + by) % size) for i in range(size)])


def on_device(child_update, block_maps, sep_share, coupling_share):
    leaf = lax.axis_index("leaf")
    rid = lax.axis_index("rows")
    core = leaf & 1
    sep = sep_share[0]
    cpl = coupling_share[0]
    where = jnp.stack([rid, core]).astype(jnp.int32)

    tie = lax.optimization_barrier
    give, keep, child = pack_shares(0, where, sep, cpl, child_update[0])
    own = jnp.concatenate([keep + swap(give, 0), child], axis=1)
    own, after = tie((own, where))
    left = shift(own, 1)
    right = shift(own, -1)

    give, keep = pack_shares(1, after, sep, cpl)
    p1 = keep + swap(give, 0)
    got = swap(p1, 1)
    give, keep = pack_shares(2, after, sep, cpl)
    p2 = keep + swap(give, 0)
    p1, p2 = p1 + got, p2 + swap(p2, 1)
    p2 = p2 + swap(p2, 2)

    opp = [shift(left[:64], 1), shift(right[64:], -1)]
    far = [swap(x, 0) for x in (own, left, right)]
    opp, far, p1, p2 = tie((opp, far, p1, p2))
    near = [own, left, right] + opp
    far = far + [swap(x, 0) for x in opp]
    mine = [None] + [lax.all_gather(p, "rows", axis=0, tiled=False) for p in (p1, p2)]

    l_all = r_all = current = give = None
    for level in range(LEVELS):
        me = leaf >> level
        child_ids = (me - core, me - core + 1) if level == 0 else (me, me ^ 1)
        ids = jnp.concatenate(
            [lax.dynamic_index_in_dim(block_maps[level], i, 0, keepdims=False) for i in child_ids] + [where]
        )
        if level == 0:
            l_all, r_all, current, give = front(0, ids, *near, *far)
            mine[1], give = tie((mine[1], give))
            continue
        got = swap(give, level)
        inputs = (mine[level], swap(mine[level], 0), current, got, swap(got, 0), l_all, r_all)
        if level == 1:
            l_all, r_all, current, give = front(1, ids, *inputs)
            mine[2], give = tie((mine[2], give))
        else:
            l_all, r_all, top = front(2, ids, *inputs)
    return l_all[None], r_all[None], top[None]


def solution(mesh):
    return jax.shard_map(
        on_device,
        mesh=mesh,
        in_specs=(
            P("leaf", "rows", None),
            P(),
            P("leaf", None, "rows", None),
            P("leaf", None, "rows", None),
        ),
        out_specs=(
            P("leaf", None, "rows", None),
            P("leaf", None, "rows", None),
            P("leaf", "rows", None),
        ),
        check_vma=False,
    )
```

```python
import jax
import jax.numpy as jnp
from jax import lax
from jax.experimental import pallas as pl
from jax.experimental.pallas import tpu as pltpu
from jax.sharding import PartitionSpec as P

BLK = 128
SEP = 1024
UPD = 512
FRONT = SEP + UPD
LEVELS = 3
NSEP = SEP // BLK
NUPD = UPD // BLK
PART = 8
PAIR = 2 * BLK
CHUNK = 4
HALVES = (((0, 0), (1, 0), (1, 1), (2, 0), (2, 1)), ((2, 2), (3, 0), (3, 1), (3, 2), (3, 3)))
f32 = jnp.float32
bf16 = jnp.bfloat16


def lane_b(x, c):
    return jnp.broadcast_to(x[:, c : c + 1], x.shape)


def sub_b(x, i):
    return jnp.broadcast_to(x[i : i + 1, :], x.shape)


def block_inverse(rows_a):
    groups = BLK // 8
    row = lax.broadcasted_iota(jnp.int32, (8, BLK), 0)
    lane = lax.broadcasted_iota(jnp.int32, (8, BLK), 1)
    M = list(rows_a)
    out = []
    for s in range(0, groups, PART):
        e = s + PART
        cols = [lane_b(M[s], 8 * s + j) for j in range(8)]
        zrows = []
        for b in range(s, e):
            c0 = 8 * b
            inside = (lane >= c0) & (lane < c0 + 8)
            coef = {g: [lane_b(M[g], c0 + k) for k in range(8)] for g in range(b + 1, e)}
            following = [lane_b(M[b + 1], c0 + 8 + j) for j in range(8)] if b + 1 < e else None
            X = jnp.where(inside, jnp.where(lane - c0 == row, 1.0, 0.0), M[b])
            rs = []
            zs = []
            ls = [[None] * 8 for _ in range(8)]
            pivot = sub_b(cols[0], 0)
            for k in range(8):
                r = lax.rsqrt(pivot)
                rs.append(r)
                if k < 7:
                    below = sub_b(cols[k], k + 1) * r
                    pivot = sub_b(cols[k + 1], k + 1) - below * below
                c = cols[k] * r
                for j in range(k + 1, 8):
                    ls[j][k] = sub_b(c, j)
                    cols[j] = cols[j] - c * ls[j][k]
                z = sub_b(X, k) * r
                zs.append(z)
                if k < 7:
                    X = X - jnp.where(row > k, c, 0.0) * z
            for g in range(b + 1, e):
                cg = coef[g]
                for k in range(8):
                    cg[k] = cg[k] * rs[k]
                    for i in range(k + 1, 8):
                        cg[i] = cg[i] - ls[i][k] * cg[k]
                m = jnp.where(inside, 0.0, M[g])
                for k in range(8):
                    m = m - cg[k] * zs[k]
                M[g] = m
                if g == b + 1:
                    for k in range(8):
                        for j in range(8):
                            following[j] = following[j] - cg[k] * sub_b(cg[k], j)
                    cols = following
            y = zs[0]
            for k in range(1, 8):
                y = jnp.where(row == k, zs[k], y)
            zrows.append(jnp.where((lane < c0 + 8) | (lane >= 8 * e), y, 0.0))
            out.append(jnp.where(lane < c0 + 8, y, 0.0))
        if e < groups:
            zh, zl = split(jnp.concatenate(zrows, axis=0))
            lhs = jnp.concatenate([zh, zh, zl], axis=0)[:, 8 * e :]
            rhs = jnp.concatenate([zh, zl, zh], axis=0)
            upd = lax.dot_general(lhs, rhs, (((0,), (0,)), ((), ())), preferred_element_type=f32)
            done = (lane >= 8 * s) & (lane < 8 * e)
            for g in range(e, groups):
                M[g] = jnp.where(done, 0.0, M[g]) - upd[8 * (g - e) : 8 * (g - e) + 8, :]
    return out


def split(x):
    hi = x.astype(bf16)
    return hi, (x - hi.astype(f32)).astype(bf16)


def nt(a, b):
    return lax.dot_general(a, b, (((1,), (1,)), ((), ())), preferred_element_type=f32)


def stack_split(x):
    hi, lo = split(x)
    rows = x.shape[0] // BLK
    parts = []
    for i in range(rows):
        parts += [hi[i * BLK : (i + 1) * BLK], lo[i * BLK : (i + 1) * BLK]]
    return jnp.concatenate(parts, axis=0)


def nt4(a, b):
    p = nt(a, b)
    rows = []
    for i in range(a.shape[0] // PAIR):
        cols = []
        for j in range(b.shape[0] // PAIR):
            q = p[i * PAIR : (i + 1) * PAIR, j * PAIR : (j + 1) * PAIR]
            cols.append(q[:BLK, :BLK] + (q[:BLK, BLK:] + q[BLK:, :BLK]) + q[BLK:, BLK:])
        rows.append(cols[0] if len(cols) == 1 else jnp.concatenate(cols, axis=1))
    return rows[0] if len(rows) == 1 else jnp.concatenate(rows, axis=0)


def blk(i):
    if isinstance(i, int):
        return pl.ds(i * BLK, BLK)
    return pl.ds(pl.multiple_of(i * BLK, BLK), BLK)


def two(i, n=1):
    if isinstance(i, int):
        return pl.ds(i * PAIR, n * PAIR)
    return pl.ds(pl.multiple_of(i * PAIR, PAIR), n * PAIR)


def chunks(lo):
    first = lo // BLK
    for i in range(first, FRONT // BLK, CHUNK):
        yield i, min(CHUNK, FRONT // BLK - i)


def front_body(level, refs):
    last = level == LEVELS - 1
    ids = refs[0]
    if level == 0:
        pieces, refs = refs[1:11], refs[11:]
    else:
        mine, theirs, own_in, near_in, far_in = refs[1:6]
        refs = refs[8:]
    l_all, r_all, u_out = refs[:3]
    refs = refs[3:]
    if not last:
        give_out, refs = refs[0], refs[1:]
    F, G, C, UG, Ub, LL, Lf, T, D, E, WW, Lo, Ro, Uo, sem = refs
    rid = ids[8]
    core = ids[9]
    copies = []

    def take(src, r, half, lo, hi):
        i = 2 * r + half
        copies.append((src.at[:, pl.ds(0, 640)], G.at[i, pl.ds(lo, hi - lo), :]))
        at = pl.multiple_of(SEP + r * BLK + half * 64, 64)
        for side in range(2):
            if lo <= side * 64 < hi:
                copies.append(
                    (src.at[pl.ds(side * 64 - lo, 64), pl.ds(640, 512)], F.at[pl.ds(at, 64), pl.ds(side * 512, 512)])
                )
        if level == 0:
            copies.append((src.at[:, pl.ds(1152, 384)], UG.at[half, r, pl.ds(lo, hi - lo), :]))

    if level == 0:
        for n, half in ((0, core), (5, 1 - core)):
            take(pieces[n], rid, half, 0, BLK)
            take(pieces[n + 1], (rid + 3) % 4, half, 0, BLK)
            take(pieces[n + 2], (rid + 1) % 4, half, 0, BLK)
            take(pieces[n + 3], (rid + 2) % 4, half, 0, 64)
            take(pieces[n + 4], (rid + 2) % 4, half, 64, BLK)
    else:
        for src, half in ((mine, core), (theirs, 1 - core)):
            for r in range(4):
                take(src.at[r], r, half, 0, BLK)
        copies.append((own_in, UG.at[0]))
        copies.append((near_in, UG.at[1, core]))
        copies.append((far_in, UG.at[1, 1 - core]))
    copies = [pltpu.make_async_copy(s, t, sem.at[n]) for n, (s, t) in enumerate(copies)]
    for c in copies:
        c.start()
    C[...] = jnp.zeros_like(C)
    LL[...] = jnp.zeros_like(LL)
    T[...] = jnp.zeros_like(T)
    WW[...] = jnp.zeros_like(WW)
    for c in copies:
        c.wait()
    for i in range(NSEP):
        for d in range(5):
            j = (i - d) % NSEP
            part = G[i, :, BLK * d : BLK * d + BLK]
            if i >= j:
                F[blk(i), blk(j)] = part
            elif d < 4:
                F[blk(j), blk(i)] = part.T
    for child in range(2):
        parts = {}
        if level == 0:
            for r in range(NUPD):
                for d in range(3):
                    if d < 2 or r >= 2:
                        parts[r, (r - d) % NUPD] = UG[child, r, :, BLK * d : BLK * d + BLK]
        else:
            for half in range(2):
                for n, ij in enumerate(HALVES[half]):
                    parts[ij] = UG[child, half, :, BLK * n : BLK * n + BLK]
        for (i, j), part in parts.items():
            Ub[child, blk(i), blk(j)] = part
            if i != j:
                Ub[child, blk(j), blk(i)] = part.T

    def add_block(t, c):
        child = t // 10
        p = t % 10
        i = (p >= 1).astype(jnp.int32) + (p >= 3).astype(jnp.int32) + (p >= 6).astype(jnp.int32)
        j = p - i * (i + 1) // 2
        mi = ids[4 * child + i]
        mj = ids[4 * child + j]
        si = jnp.where(mi >= mj, i, j)
        sj = i + j - si
        hi = jnp.maximum(mi, mj)
        lo = jnp.minimum(mi, mj)

        @pl.when(lo < NSEP)
        def _():
            F[blk(hi), blk(lo)] += Ub[child, blk(si), blk(sj)]

        @pl.when(lo >= NSEP)
        def _():
            h = jnp.maximum(hi - NSEP, 0)
            l = jnp.maximum(lo - NSEP, 0)
            C[blk(h), blk(l)] += Ub[child, blk(si), blk(sj)]
            if last:

                @pl.when(i > j)
                def _():
                    C[blk(l), blk(h)] += Ub[child, blk(sj), blk(si)]

        return c

    lax.fori_loop(0, 20, add_block, 0)
    D[...] = F[:BLK, :BLK]

    def panel(k, lo):
        for i, n in chunks(lo):
            rows = pl.ds(i * BLK, n * BLK)
            v = nt4(stack_split(T[rows, :]), WW[...])
            Lf[rows, blk(k)] = v
            LL[two(i, n), blk(k)] = stack_split(v)

    def step(k, lo, depth):
        nxt = jnp.minimum(k + 1, NSEP - 1)
        panel(jnp.maximum(k - 1, 0), lo)
        for i, n in chunks(lo):
            rows = pl.ds(i * BLK, n * BLK)
            T[rows, :] = F[rows, blk(k)] - nt4(LL[two(i, n), :depth], LL[two(k), :depth])
        near = LL[two(nxt), :depth]
        E[...] = F[blk(nxt), blk(nxt)] - nt4(near, near)
        W = jnp.concatenate(block_inverse([D[8 * g : 8 * g + 8, :] for g in range(BLK // 8)]), axis=0)
        WW[...] = stack_split(W)
        l = stack_split(nt4(stack_split(T[blk(nxt), :]), WW[...]))
        D[...] = E[...] - nt4(l, l)

    lax.fori_loop(0, 4, lambda k, c: (step(k, 0, 384), c)[1], 0)
    lax.fori_loop(4, 8, lambda k, c: (step(k, 384, 896), c)[1], 0)
    panel(7, 896)
    rows = pl.ds(pl.multiple_of(rid * 256, 256), 256)
    ri = lax.broadcasted_iota(jnp.int32, (256, SEP), 0) + rid * 256
    ci = lax.broadcasted_iota(jnp.int32, (256, SEP), 1)
    Lo[...] = jnp.where(ri >= ci, Lf[rows, :], 0.0)
    Ro[...] = Lf[pl.ds(pl.multiple_of(SEP + rid * BLK, BLK), BLK), :]
    writes = [
        pltpu.make_async_copy(Lo, l_all.at[level], sem.at[0]),
        pltpu.make_async_copy(Ro, r_all.at[level], sem.at[1]),
    ]
    for c in writes:
        c.start()
    if last:
        mine_u = pl.ds(pl.multiple_of(rid * BLK, BLK), BLK)
        u_out[...] = C[mine_u, :] - nt4(LL[two(NSEP + rid), :], LL[two(NSEP, NUPD), :])
    else:
        place = {ij: (half, n) for half in range(2) for n, ij in enumerate(HALVES[half])}
        for i in range(NUPD):
            new = C[blk(i), : BLK * (i + 1)] - nt4(LL[two(NSEP + i), :], LL[two(NSEP, i + 1), :])
            for j in range(i + 1):
                half, n = place[i, j]
                Uo[half, :, BLK * n : BLK * n + BLK] = new[:, BLK * j : BLK * j + BLK]
        writes += [
            pltpu.make_async_copy(Uo, u_out, sem.at[2]),
            pltpu.make_async_copy(Uo.at[core], give_out, sem.at[3]),
        ]
        for c in writes[2:]:
            c.start()
    for c in writes:
        c.wait()


def front(level, ids, *inputs):
    smem = pl.BlockSpec(memory_space=pltpu.SMEM)
    vmem = pl.BlockSpec(memory_space=pltpu.VMEM)
    hbm = pl.BlockSpec(memory_space=pltpu.HBM)
    last = level == LEVELS - 1
    update = [(BLK, UPD)] if last else [(2, BLK, 640), (BLK, 640)]
    shapes = [(LEVELS, 256, SEP), (LEVELS, BLK, SEP)] + update
    return pl.pallas_call(
        lambda *refs: front_body(level, refs),
        in_specs=[smem] + [hbm] * len(inputs),
        out_specs=[hbm] * 2 + ([vmem] if last else [hbm] * 2),
        out_shape=[jax.ShapeDtypeStruct(s, f32) for s in shapes],
        input_output_aliases={} if level == 0 else {6: 0, 7: 1},
        scratch_shapes=[
            pltpu.VMEM((FRONT, SEP), f32),
            pltpu.VMEM((NSEP, BLK, 640), f32),
            pltpu.VMEM((UPD, UPD), f32),
            pltpu.VMEM((2, 4, BLK, 384) if level == 0 else (2, 2, BLK, 640), f32),
            pltpu.VMEM((2, UPD, UPD), f32),
            pltpu.VMEM((2 * FRONT, SEP), bf16),
            pltpu.VMEM((FRONT, SEP), f32),
            pltpu.VMEM((FRONT, BLK), f32),
            pltpu.VMEM((BLK, BLK), f32),
            pltpu.VMEM((BLK, BLK), f32),
            pltpu.VMEM((PAIR, BLK), bf16),
            pltpu.VMEM((256, SEP), f32),
            pltpu.VMEM((BLK, SEP), f32),
            pltpu.VMEM((2, BLK, 640), f32),
            pltpu.SemaphoreType.DMA((40,)),
        ],
        compiler_params=pltpu.CompilerParams(vmem_limit_bytes=60 << 20),
        cost_estimate=pl.CostEstimate(flops=20_000_000_000, transcendentals=0, bytes_accessed=20_000_000),
        name=f"front{level}",
    )(ids, *inputs)


def pack_body(ids, sep, cpl, child, *outs):
    rid = ids[0]
    core = ids[1]
    for d in range(3):
        outs[0][:, BLK * d : BLK * d + BLK] = child[:, blk((rid + NUPD - d) % NUPD)]
    for level in range(LEVELS):
        for out, half in ((outs[1 + 2 * level], 1 - core), (outs[2 + 2 * level], core)):
            i = 2 * rid + half
            rows = pl.ds(pl.multiple_of(half * BLK, BLK), BLK)
            for d in range(5):
                out[:, BLK * d : BLK * d + BLK] = sep[level, rows, blk((i + NSEP - d) % NSEP)]
            for side in range(2):
                at = pl.ds(pl.multiple_of(half * 64, 64), 64)
                out[64 * side : 64 * side + 64, 640:] = cpl[level, at, 512 * side : 512 * side + 512]


def pack_shares(ids, sep, cpl, child):
    vmem = pl.BlockSpec(memory_space=pltpu.VMEM)
    return pl.pallas_call(
        pack_body,
        in_specs=[pl.BlockSpec(memory_space=pltpu.SMEM)] + [vmem] * 3,
        out_specs=[vmem] * 7,
        out_shape=[jax.ShapeDtypeStruct((BLK, 384), f32)] + [jax.ShapeDtypeStruct((BLK, 1152), f32)] * 6,
        compiler_params=pltpu.CompilerParams(vmem_limit_bytes=24 << 20),
        name="pack",
    )(ids, sep, cpl, child)


def swap(x, stride):
    return lax.ppermute(x, "leaf", [(i, i ^ 1 << stride) for i in range(lax.axis_size("leaf"))])


def shift(x, by):
    size = lax.axis_size("rows")
    return lax.ppermute(x, "rows", [(i, (i + by) % size) for i in range(size)])


def turn(x, by):
    return lax.ppermute(x, "leaf", [(i, i ^ (by << 1)) for i in range(lax.axis_size("leaf"))])


def on_device(child_update, block_maps, sep_share, coupling_share):
    leaf = lax.axis_index("leaf")
    rid = lax.axis_index("rows")
    core = leaf & 1
    sep = sep_share[0]
    cpl = coupling_share[0]
    where = jnp.stack([rid, core]).astype(jnp.int32)

    tie = lax.optimization_barrier
    tie = lax.optimization_barrier
    child, give0, keep0, give1, keep1, give2, keep2 = pack_shares(where, sep, cpl, child_update[0])
    own = jnp.concatenate([keep0 + swap(give0, 0), child], axis=1)
    left = shift(own, 1)
    right = shift(own, -1)
    p1 = keep1 + swap(give1, 0)
    p1 = p1 + swap(p1, 1)
    p2 = keep2 + swap(give2, 0)
    opp = [shift(left[:64], 1), shift(right[64:], -1)]
    far = [swap(x, 0) for x in (own, left, right)]
    opp, far, p1, p2 = tie((opp, far, p1, p2))
    near = [own, left, right] + opp
    far = far + [swap(x, 0) for x in opp]
    mine = [None, lax.all_gather(p1, "rows", axis=0, tiled=False), None]
    others = [turn(p2, by) for by in (1, 2, 3)]

    l_all = r_all = current = give = None
    for level in range(LEVELS):
        me = leaf >> level
        child_ids = (me - core, me - core + 1) if level == 0 else (me, me ^ 1)
        ids = jnp.concatenate(
            [lax.dynamic_index_in_dim(block_maps[level], i, 0, keepdims=False) for i in child_ids] + [where]
        )
        if level == 0:
            l_all, r_all, current, give = front(0, ids, *near, *far)
            p2, mine[1], current, give = tie((p2, mine[1], current, give))
            mine[2] = lax.all_gather(p2 + others[0] + others[1] + others[2], "rows", axis=0, tiled=False)
            continue
        got = swap(give, level)
        inputs = (mine[level], swap(mine[level], 0), current, got, swap(got, 0), l_all, r_all)
        if level == 1:
            l_all, r_all, current, give = front(1, ids, *inputs)
            mine[2], give = tie((mine[2], give))
        else:
            l_all, r_all, top = front(2, ids, *inputs)
    return l_all[None], r_all[None], top[None]


def solution(mesh):
    return jax.shard_map(
        on_device,
        mesh=mesh,
        in_specs=(
            P("leaf", "rows", None),
            P(),
            P("leaf", None, "rows", None),
            P("leaf", None, "rows", None),
        ),
        out_specs=(
            P("leaf", None, "rows", None),
            P("leaf", None, "rows", None),
            P("leaf", "rows", None),
        ),
        check_vma=False,
    )
```

```python
import jax
import jax.numpy as jnp
from jax import lax
from jax.experimental import pallas as pl
from jax.experimental.pallas import tpu as pltpu
from jax.sharding import PartitionSpec as P

BLK = 128
SEP = 1024
UPD = 512
FRONT = SEP + UPD
LEVELS = 3
NSEP = SEP // BLK
NUPD = UPD // BLK
PART = 8
PAIR = 2 * BLK
CHUNK = 4
HALVES = (((0, 0), (1, 0), (1, 1), (2, 0), (2, 1)), ((2, 2), (3, 0), (3, 1), (3, 2), (3, 3)))
f32 = jnp.float32
bf16 = jnp.bfloat16


def lane_b(x, c):
    return jnp.broadcast_to(x[:, c : c + 1], x.shape)


def sub_b(x, i):
    return jnp.broadcast_to(x[i : i + 1, :], x.shape)


def block_inverse(rows_a):
    groups = BLK // 8
    row = lax.broadcasted_iota(jnp.int32, (8, BLK), 0)
    lane = lax.broadcasted_iota(jnp.int32, (8, BLK), 1)
    M = list(rows_a)
    out = []
    for s in range(0, groups, PART):
        e = s + PART
        cols = [lane_b(M[s], 8 * s + j) for j in range(8)]
        zrows = []
        for b in range(s, e):
            c0 = 8 * b
            inside = (lane >= c0) & (lane < c0 + 8)
            coef = {g: [lane_b(M[g], c0 + k) for k in range(8)] for g in range(b + 1, e)}
            following = [lane_b(M[b + 1], c0 + 8 + j) for j in range(8)] if b + 1 < e else None
            X = jnp.where(inside, jnp.where(lane - c0 == row, 1.0, 0.0), M[b])
            rs = []
            zs = []
            ls = [[None] * 8 for _ in range(8)]
            pivot = sub_b(cols[0], 0)
            for k in range(8):
                r = lax.rsqrt(pivot)
                rs.append(r)
                if k < 7:
                    below = sub_b(cols[k], k + 1) * r
                    pivot = sub_b(cols[k + 1], k + 1) - below * below
                c = cols[k] * r
                for j in range(k + 1, 8):
                    ls[j][k] = sub_b(c, j)
                    cols[j] = cols[j] - c * ls[j][k]
                z = sub_b(X, k) * r
                zs.append(z)
                if k < 7:
                    X = X - jnp.where(row > k, c, 0.0) * z
            for g in range(b + 1, e):
                cg = coef[g]
                for k in range(8):
                    cg[k] = cg[k] * rs[k]
                    for i in range(k + 1, 8):
                        cg[i] = cg[i] - ls[i][k] * cg[k]
                m = jnp.where(inside, 0.0, M[g])
                for k in range(8):
                    m = m - cg[k] * zs[k]
                M[g] = m
                if g == b + 1:
                    for k in range(8):
                        for j in range(8):
                            following[j] = following[j] - cg[k] * sub_b(cg[k], j)
                    cols = following
            y = zs[0]
            for k in range(1, 8):
                y = jnp.where(row == k, zs[k], y)
            zrows.append(jnp.where((lane < c0 + 8) | (lane >= 8 * e), y, 0.0))
            out.append(jnp.where(lane < c0 + 8, y, 0.0))
        if e < groups:
            zh, zl = split(jnp.concatenate(zrows, axis=0))
            lhs = jnp.concatenate([zh, zh, zl], axis=0)[:, 8 * e :]
            rhs = jnp.concatenate([zh, zl, zh], axis=0)
            upd = lax.dot_general(lhs, rhs, (((0,), (0,)), ((), ())), preferred_element_type=f32)
            done = (lane >= 8 * s) & (lane < 8 * e)
            for g in range(e, groups):
                M[g] = jnp.where(done, 0.0, M[g]) - upd[8 * (g - e) : 8 * (g - e) + 8, :]
    return out


def split(x):
    hi = x.astype(bf16)
    return hi, (x - hi.astype(f32)).astype(bf16)


def nt(a, b):
    return lax.dot_general(a, b, (((1,), (1,)), ((), ())), preferred_element_type=f32)


def stack_split(x):
    hi, lo = split(x)
    rows = x.shape[0] // BLK
    parts = []
    for i in range(rows):
        parts += [hi[i * BLK : (i + 1) * BLK], lo[i * BLK : (i + 1) * BLK]]
    return jnp.concatenate(parts, axis=0)


def nt4(a, b):
    p = nt(a, b)
    rows = []
    for i in range(a.shape[0] // PAIR):
        cols = []
        for j in range(b.shape[0] // PAIR):
            q = p[i * PAIR : (i + 1) * PAIR, j * PAIR : (j + 1) * PAIR]
            cols.append(q[:BLK, :BLK] + (q[:BLK, BLK:] + q[BLK:, :BLK]) + q[BLK:, BLK:])
        rows.append(cols[0] if len(cols) == 1 else jnp.concatenate(cols, axis=1))
    return rows[0] if len(rows) == 1 else jnp.concatenate(rows, axis=0)


def blk(i):
    if isinstance(i, int):
        return pl.ds(i * BLK, BLK)
    return pl.ds(pl.multiple_of(i * BLK, BLK), BLK)


def two(i, n=1):
    if isinstance(i, int):
        return pl.ds(i * PAIR, n * PAIR)
    return pl.ds(pl.multiple_of(i * PAIR, PAIR), n * PAIR)


def chunks(lo):
    first = lo // BLK
    for i in range(first, FRONT // BLK, CHUNK):
        yield i, min(CHUNK, FRONT // BLK - i)


def front_body(level, refs):
    last = level == LEVELS - 1
    ids = refs[0]
    if level == 0:
        pieces, refs = refs[1:11], refs[11:]
    else:
        mine, theirs, own_in, near_in, far_in = refs[1:6]
        refs = refs[8:]
    l_all, r_all, u_out = refs[:3]
    refs = refs[3:]
    if not last:
        give_out, refs = refs[0], refs[1:]
    F, G, C, UG, Ub, LL, Lf, T, D, E, WW, Lo, Ro, Uo, sem = refs
    rid = ids[8]
    core = ids[9]
    copies = []

    def take(src, r, half, lo, hi):
        i = 2 * r + half
        copies.append((src.at[:, pl.ds(0, 640)], G.at[i, pl.ds(lo, hi - lo), :]))
        at = pl.multiple_of(SEP + r * BLK + half * 64, 64)
        for side in range(2):
            if lo <= side * 64 < hi:
                copies.append(
                    (src.at[pl.ds(side * 64 - lo, 64), pl.ds(640, 512)], F.at[pl.ds(at, 64), pl.ds(side * 512, 512)])
                )
        if level == 0:
            copies.append((src.at[:, pl.ds(1152, 384)], UG.at[half, r, pl.ds(lo, hi - lo), :]))

    if level == 0:
        for n, half in ((0, core), (5, 1 - core)):
            take(pieces[n], rid, half, 0, BLK)
            take(pieces[n + 1], (rid + 3) % 4, half, 0, BLK)
            take(pieces[n + 2], (rid + 1) % 4, half, 0, BLK)
            take(pieces[n + 3], (rid + 2) % 4, half, 0, 64)
            take(pieces[n + 4], (rid + 2) % 4, half, 64, BLK)
    else:
        for src, half in ((mine, core), (theirs, 1 - core)):
            for r in range(4):
                take(src.at[r], r, half, 0, BLK)
        copies.append((own_in, UG.at[0]))
        copies.append((near_in, UG.at[1, core]))
        copies.append((far_in, UG.at[1, 1 - core]))
    copies = [pltpu.make_async_copy(s, t, sem.at[n]) for n, (s, t) in enumerate(copies)]
    for c in copies:
        c.start()
    C[...] = jnp.zeros_like(C)
    LL[...] = jnp.zeros_like(LL)
    T[...] = jnp.zeros_like(T)
    WW[...] = jnp.zeros_like(WW)
    for c in copies:
        c.wait()
    for i in range(NSEP):
        for d in range(5):
            j = (i - d) % NSEP
            part = G[i, :, BLK * d : BLK * d + BLK]
            if i >= j:
                F[blk(i), blk(j)] = part
            elif d < 4:
                F[blk(j), blk(i)] = part.T
    for child in range(2):
        parts = {}
        if level == 0:
            for r in range(NUPD):
                for d in range(3):
                    if d < 2 or r >= 2:
                        parts[r, (r - d) % NUPD] = UG[child, r, :, BLK * d : BLK * d + BLK]
        else:
            for half in range(2):
                for n, ij in enumerate(HALVES[half]):
                    parts[ij] = UG[child, half, :, BLK * n : BLK * n + BLK]
        for (i, j), part in parts.items():
            Ub[child, blk(i), blk(j)] = part
            if i != j:
                Ub[child, blk(j), blk(i)] = part.T

    def add_block(t, c):
        child = t // 10
        p = t % 10
        i = (p >= 1).astype(jnp.int32) + (p >= 3).astype(jnp.int32) + (p >= 6).astype(jnp.int32)
        j = p - i * (i + 1) // 2
        mi = ids[4 * child + i]
        mj = ids[4 * child + j]
        si = jnp.where(mi >= mj, i, j)
        sj = i + j - si
        hi = jnp.maximum(mi, mj)
        lo = jnp.minimum(mi, mj)

        @pl.when(lo < NSEP)
        def _():
            F[blk(hi), blk(lo)] += Ub[child, blk(si), blk(sj)]

        @pl.when(lo >= NSEP)
        def _():
            h = jnp.maximum(hi - NSEP, 0)
            l = jnp.maximum(lo - NSEP, 0)
            C[blk(h), blk(l)] += Ub[child, blk(si), blk(sj)]
            if last:

                @pl.when(i > j)
                def _():
                    C[blk(l), blk(h)] += Ub[child, blk(sj), blk(si)]

        return c

    lax.fori_loop(0, 20, add_block, 0)
    D[...] = F[:BLK, :BLK]

    def panel(k, lo):
        for i, n in chunks(lo):
            rows = pl.ds(i * BLK, n * BLK)
            v = nt4(stack_split(T[rows, :]), WW[...])
            Lf[rows, blk(k)] = v
            LL[two(i, n), blk(k)] = stack_split(v)

    def step(k, lo, depth):
        nxt = jnp.minimum(k + 1, NSEP - 1)
        panel(jnp.maximum(k - 1, 0), lo)
        for i, n in chunks(lo):
            rows = pl.ds(i * BLK, n * BLK)
            T[rows, :] = F[rows, blk(k)] - nt4(LL[two(i, n), :depth], LL[two(k), :depth])
        near = LL[two(nxt), :depth]
        E[...] = F[blk(nxt), blk(nxt)] - nt4(near, near)
        W = jnp.concatenate(block_inverse([D[8 * g : 8 * g + 8, :] for g in range(BLK // 8)]), axis=0)
        WW[...] = stack_split(W)
        wh, wl = split(W)
        th, tl = split(T[blk(nxt), :])
        v = nt(jnp.concatenate([th, th, tl], axis=1), jnp.concatenate([wh, wl, wh], axis=1))
        h, l = split(v)
        D[...] = E[...] - nt(jnp.concatenate([h, h, l], axis=1), jnp.concatenate([h, l, h], axis=1))

    lax.fori_loop(0, 4, lambda k, c: (step(k, 0, 384), c)[1], 0)
    lax.fori_loop(4, 8, lambda k, c: (step(k, 384, 896), c)[1], 0)
    panel(7, 896)
    rows = pl.ds(pl.multiple_of(rid * 256, 256), 256)
    ri = lax.broadcasted_iota(jnp.int32, (256, SEP), 0) + rid * 256
    ci = lax.broadcasted_iota(jnp.int32, (256, SEP), 1)
    Lo[...] = jnp.where(ri >= ci, Lf[rows, :], 0.0)
    Ro[...] = Lf[pl.ds(pl.multiple_of(SEP + rid * BLK, BLK), BLK), :]
    writes = [
        pltpu.make_async_copy(Lo, l_all.at[level], sem.at[0]),
        pltpu.make_async_copy(Ro, r_all.at[level], sem.at[1]),
    ]
    for c in writes:
        c.start()
    if last:
        mine_u = pl.ds(pl.multiple_of(rid * BLK, BLK), BLK)
        u_out[...] = C[mine_u, :] - nt4(LL[two(NSEP + rid), :], LL[two(NSEP, NUPD), :])
    else:
        place = {ij: (half, n) for half in range(2) for n, ij in enumerate(HALVES[half])}
        for i in range(NUPD):
            new = C[blk(i), : BLK * (i + 1)] - nt4(LL[two(NSEP + i), :], LL[two(NSEP, i + 1), :])
            for j in range(i + 1):
                half, n = place[i, j]
                Uo[half, :, BLK * n : BLK * n + BLK] = new[:, BLK * j : BLK * j + BLK]
        writes += [
            pltpu.make_async_copy(Uo, u_out, sem.at[2]),
            pltpu.make_async_copy(Uo.at[core], give_out, sem.at[3]),
        ]
        for c in writes[2:]:
            c.start()
    for c in writes:
        c.wait()


def front(level, ids, *inputs):
    smem = pl.BlockSpec(memory_space=pltpu.SMEM)
    vmem = pl.BlockSpec(memory_space=pltpu.VMEM)
    hbm = pl.BlockSpec(memory_space=pltpu.HBM)
    last = level == LEVELS - 1
    update = [(BLK, UPD)] if last else [(2, BLK, 640), (BLK, 640)]
    shapes = [(LEVELS, 256, SEP), (LEVELS, BLK, SEP)] + update
    return pl.pallas_call(
        lambda *refs: front_body(level, refs),
        in_specs=[smem] + [hbm] * len(inputs),
        out_specs=[hbm] * 2 + ([vmem] if last else [hbm] * 2),
        out_shape=[jax.ShapeDtypeStruct(s, f32) for s in shapes],
        input_output_aliases={} if level == 0 else {6: 0, 7: 1},
        scratch_shapes=[
            pltpu.VMEM((FRONT, SEP), f32),
            pltpu.VMEM((NSEP, BLK, 640), f32),
            pltpu.VMEM((UPD, UPD), f32),
            pltpu.VMEM((2, 4, BLK, 384) if level == 0 else (2, 2, BLK, 640), f32),
            pltpu.VMEM((2, UPD, UPD), f32),
            pltpu.VMEM((2 * FRONT, SEP), bf16),
            pltpu.VMEM((FRONT, SEP), f32),
            pltpu.VMEM((FRONT, BLK), f32),
            pltpu.VMEM((BLK, BLK), f32),
            pltpu.VMEM((BLK, BLK), f32),
            pltpu.VMEM((PAIR, BLK), bf16),
            pltpu.VMEM((256, SEP), f32),
            pltpu.VMEM((BLK, SEP), f32),
            pltpu.VMEM((2, BLK, 640), f32),
            pltpu.SemaphoreType.DMA((40,)),
        ],
        compiler_params=pltpu.CompilerParams(vmem_limit_bytes=63 << 20),
        cost_estimate=pl.CostEstimate(flops=20_000_000_000, transcendentals=0, bytes_accessed=20_000_000),
        name=f"front{level}",
    )(ids, *inputs)


def pack_body(ids, sep, cpl, child, *outs):
    rid = ids[0]
    core = ids[1]
    for d in range(3):
        outs[0][:, BLK * d : BLK * d + BLK] = child[:, blk((rid + NUPD - d) % NUPD)]
    for level in range(LEVELS):
        for out, half in ((outs[1 + 2 * level], 1 - core), (outs[2 + 2 * level], core)):
            i = 2 * rid + half
            rows = pl.ds(pl.multiple_of(half * BLK, BLK), BLK)
            for d in range(5):
                out[:, BLK * d : BLK * d + BLK] = sep[level, rows, blk((i + NSEP - d) % NSEP)]
            for side in range(2):
                at = pl.ds(pl.multiple_of(half * 64, 64), 64)
                out[64 * side : 64 * side + 64, 640:] = cpl[level, at, 512 * side : 512 * side + 512]


def pack_shares(ids, sep, cpl, child):
    vmem = pl.BlockSpec(memory_space=pltpu.VMEM)
    return pl.pallas_call(
        pack_body,
        in_specs=[pl.BlockSpec(memory_space=pltpu.SMEM)] + [vmem] * 3,
        out_specs=[vmem] * 7,
        out_shape=[jax.ShapeDtypeStruct((BLK, 384), f32)] + [jax.ShapeDtypeStruct((BLK, 1152), f32)] * 6,
        compiler_params=pltpu.CompilerParams(vmem_limit_bytes=24 << 20),
        name="pack",
    )(ids, sep, cpl, child)


def swap(x, stride):
    return lax.ppermute(x, "leaf", [(i, i ^ 1 << stride) for i in range(lax.axis_size("leaf"))])


def shift(x, by):
    size = lax.axis_size("rows")
    return lax.ppermute(x, "rows", [(i, (i + by) % size) for i in range(size)])


def turn(x, by):
    return lax.ppermute(x, "leaf", [(i, i ^ (by << 1)) for i in range(lax.axis_size("leaf"))])


def on_device(child_update, block_maps, sep_share, coupling_share):
    leaf = lax.axis_index("leaf")
    rid = lax.axis_index("rows")
    core = leaf & 1
    sep = sep_share[0]
    cpl = coupling_share[0]
    where = jnp.stack([rid, core]).astype(jnp.int32)

    tie = lax.optimization_barrier
    tie = lax.optimization_barrier
    child, give0, keep0, give1, keep1, give2, keep2 = pack_shares(where, sep, cpl, child_update[0])
    own = jnp.concatenate([keep0 + swap(give0, 0), child], axis=1)
    left = shift(own, 1)
    right = shift(own, -1)
    p1 = keep1 + swap(give1, 0)
    p1 = p1 + swap(p1, 1)
    p2 = keep2 + swap(give2, 0)
    opp = [shift(left[:64], 1), shift(right[64:], -1)]
    far = [swap(x, 0) for x in (own, left, right)]
    opp, far, p1, p2 = tie((opp, far, p1, p2))
    near = [own, left, right] + opp
    far = far + [swap(x, 0) for x in opp]
    mine = [None, lax.all_gather(p1, "rows", axis=0, tiled=False), None]
    others = [turn(p2, by) for by in (1, 2, 3)]

    l_all = r_all = current = give = None
    for level in range(LEVELS):
        me = leaf >> level
        child_ids = (me - core, me - core + 1) if level == 0 else (me, me ^ 1)
        ids = jnp.concatenate(
            [lax.dynamic_index_in_dim(block_maps[level], i, 0, keepdims=False) for i in child_ids] + [where]
        )
        if level == 0:
            l_all, r_all, current, give = front(0, ids, *near, *far)
            p2, mine[1], current, give = tie((p2, mine[1], current, give))
            mine[2] = lax.all_gather(p2 + others[0] + others[1] + others[2], "rows", axis=0, tiled=False)
            continue
        got = swap(give, level)
        inputs = (mine[level], swap(mine[level], 0), current, got, swap(got, 0), l_all, r_all)
        if level == 1:
            l_all, r_all, current, give = front(1, ids, *inputs)
            mine[2], give = tie((mine[2], give))
        else:
            l_all, r_all, top = front(2, ids, *inputs)
    return l_all[None], r_all[None], top[None]


def solution(mesh):
    return jax.shard_map(
        on_device,
        mesh=mesh,
        in_specs=(
            P("leaf", "rows", None),
            P(),
            P("leaf", None, "rows", None),
            P("leaf", None, "rows", None),
        ),
        out_specs=(
            P("leaf", None, "rows", None),
            P("leaf", None, "rows", None),
            P("leaf", "rows", None),
        ),
        check_vma=False,
    )
```
